128 devices in a mesh: mode: 8 (over z, y_hi), slab: 16 (over x, y_lo, core).
Axes of the slice: x: 4, y: 4 (y_hi: 2, y_lo: 2; y = y_hi * 2 + y_lo), z: 4, core: 2. Of those that a mesh axis runs over, the one named last changes fastest.
Arguments:
- modes: bfloat16 [48, 3, 32, 256, 128], P('mode', None, 'slab'), may hold values from -100 to 100
- volume: float32 [32, 256, 128], P(None, ('mode', 'slab')), may hold values from 0.5 to 24
Outputs:
- convective: float32 [2304, 48], P(('mode', 'slab'))
- dissipation: float32 [48, 48], replicated
The draws below stay inside these ranges and needn't reach their ends.
All inputs are finite; a program needn't handle non-finite values.
Results may differ from the reference program's by a relative error of at most 0.0043.
Values may be sent and summed in bfloat16 or wider, within the bound.
A program may use at most 128 MiB of HBM per device.

```python
import math
import jax
import jax.numpy as jnp
from jax import lax

NM = 48
NZ = 128
NX = 32
NY = 256


def draw_modes(key, part):
    key_shared, key_mix, key_amp, key_noise = jax.random.split(key, 4)
    shared = jax.random.truncated_normal(key_shared, -4.0, 4.0, (4, 3, NX, NY, NZ), jnp.float32)
    mixing = 0.6 * jax.random.truncated_normal(key_mix, -2.0, 2.0, (NM, 4), jnp.float32)
    amplitude = jnp.exp(jax.random.uniform(key_amp, (NM,), jnp.float32, math.log(0.5), math.log(2.0)))

    def one_mode(mode_number):
        noise_key = jax.random.fold_in(key_noise, mode_number)
        noise_field = jax.random.truncated_normal(noise_key, -4.0, 4.0, (3, NX, NY, NZ), jnp.float32)
        mode_field = noise_field
        for shared_number in range(4):
            mode_field = mode_field + mixing[mode_number, shared_number] * shared[shared_number]
        return (amplitude[mode_number] * mode_field).astype(jnp.bfloat16)
    return lax.map(one_mode, jnp.arange(NM, dtype=jnp.int32))


def draw_volume(key, part):
    rows_ramp = jnp.exp(math.log(3.0) * jnp.arange(NY, dtype=jnp.float32) / (NY - 1))
    base = jnp.exp(jax.random.uniform(key, (NX, NY, NZ), jnp.float32, math.log(0.5), math.log(2.0)))
    return base * rows_ramp[None, :, None]


def setup_inputs(seed: int = 0) -> dict:
    key_of = jax.random.split(jax.random.key(seed), 3)
    modes = draw_modes(jax.random.fold_in(key_of[2], 71), 0)
    volume = draw_volume(jax.random.fold_in(key_of[2], 71), 0)
    return dict(modes=modes, volume=volume)


viscosity = 0.05

def stencil(padded, dim, length):
    shifted = [lax.slice_in_dim(padded, offset, offset + length, axis=dim).astype(jnp.float32) for offset in range(5)]
    return (shifted[0] - 8.0 * shifted[1] + 8.0 * shifted[3] - shifted[4]) / 12.0

def gradient_fields(centre, x_padded, y_padded):
    z_padded = jnp.concatenate([centre[..., -2:], centre, centre[..., :2]], axis=4)
    along_x = stencil(x_padded, 2, centre.shape[2])
    along_y = stencil(y_padded, 3, centre.shape[3])
    along_z = stencil(z_padded, 4, centre.shape[4])
    return jnp.stack([along_x, along_y, along_z], axis=2).astype(jnp.bfloat16)

def contract(values, grad_all, weights, limit):
    mode_count = values.shape[0]
    cell_count = weights.size
    block_size = math.gcd(cell_count, limit)
    flat_values = values.reshape(mode_count, 3, cell_count)
    flat_grads = grad_all.reshape(mode_count, 3, 3, cell_count)
    flat_weights = weights.reshape(cell_count)

    def one_step(number, running):
        first_cell = (number * block_size).astype(jnp.int32)
        piece_values = lax.dynamic_slice_in_dim(flat_values, first_cell, block_size, 2)
        piece_grads = lax.dynamic_slice_in_dim(flat_grads, first_cell, block_size, 3)
        piece_weights = lax.dynamic_slice_in_dim(flat_weights, first_cell, block_size, 0)
        values_wide = piece_values.astype(jnp.float32)
        grads_wide = piece_grads.astype(jnp.float32)
        carried = values_wide[:, None, None, 0, :] * grads_wide[None, :, :, 0, :]
        carried = carried + values_wide[:, None, None, 1, :] * grads_wide[None, :, :, 1, :]
        carried = carried + values_wide[:, None, None, 2, :] * grads_wide[None, :, :, 2, :]
        carried = (carried * piece_weights).astype(jnp.bfloat16).reshape(mode_count * mode_count, 3 * block_size)
        conv_add = lax.dot_general(piece_values.reshape(mode_count, 3 * block_size), carried, (((1,), (1,)), ((), ())), preferred_element_type=jnp.float32)
        weighted = (grads_wide * piece_weights).astype(jnp.bfloat16).reshape(mode_count, 9 * block_size)
        diss_add = lax.dot_general(piece_grads.reshape(mode_count, 9 * block_size), weighted, (((1,), (1,)), ((), ())), preferred_element_type=jnp.float32)
        return (running[0] + conv_add, running[1] + diss_add)
    start_conv = jnp.zeros((mode_count, mode_count * mode_count), jnp.float32)
    start_diss = jnp.zeros((mode_count, mode_count), jnp.float32)
    conv_sum, diss_sum = lax.fori_loop(0, cell_count // block_size, one_step, (start_conv, start_diss))
    return (conv_sum.reshape(mode_count * mode_count, mode_count), diss_sum)

def reference(modes, volume):
    row_block = math.gcd(NY, 8)
    block_total = NY // row_block
    cell_total = NX * NY * NZ

    def one_rows(running, row_number):
        first_row = (row_number * row_block).astype(jnp.int32)
        wanted = first_row - 2 + jnp.arange(row_block + 4, dtype=jnp.int32)
        inside = (wanted >= 0) & (wanted < NY)
        clipped = jnp.clip(wanted, 0, NY - 1).astype(jnp.int32)
        taken = jnp.take(modes, clipped, axis=3)
        y_padded = jnp.where(inside[None, None, None, :, None], taken, jnp.zeros((), modes.dtype))
        centre = y_padded[:, :, :, 2:-2]
        x_padded = jnp.pad(centre, ((0, 0), (0, 0), (2, 2), (0, 0), (0, 0)))
        grad_all = gradient_fields(centre, x_padded, y_padded)
        weights = lax.dynamic_slice_in_dim(volume, first_row, row_block, 1)
        conv_add, diss_add = contract(centre, grad_all, weights, 4096)
        return ((running[0] + conv_add, running[1] + diss_add), None)
    start = (jnp.zeros((NM * NM, NM), jnp.float32), jnp.zeros((NM, NM), jnp.float32))
    (conv_sum, diss_sum), unused = lax.scan(one_rows, start, jnp.arange(block_total, dtype=jnp.int32))
    convective = conv_sum * (1.0 / math.sqrt(cell_total))
    dissipation = diss_sum * (viscosity / cell_total)
    return (convective, dissipation)
```

```python
import math

import jax
import jax.numpy as jnp
from jax import lax
from jax.experimental import pallas as pl
from jax.experimental.pallas import tpu as pltpu
from jax.sharding import PartitionSpec as P

viscosity = 0.05
bf16 = jnp.bfloat16
f32 = jnp.float32
MESH = pl.DeviceIdType.MESH
NT = (((1,), (1,)), ((), ()))
GROUP = 16


def place():
    m = lax.axis_index("mode")
    s = lax.axis_index("slab")
    return s // 4, (m % 2) * 2 + (s % 4) // 2, m // 2, s % 2


def device(x, y, z, core):
    return (z * 2 + y // 2, x * 4 + (y % 2) * 2 + core)


def block_of(y, z, core):
    return 2 * (y * 4 + z + (y % 2) * (3 - 2 * z)) + core


def owner_of(q):
    step = q // 2
    y = step // 4
    along = step % 4
    return y, along + (y % 2) * (3 - 2 * along), q % 2


def main_kernel(
    modes, volume, conv, diss, recv, vrecv, uc, wide, g, gw, uv,
    send_sem, recv_sem, vsend_sem, vrecv_sem, hsend_sem, hrecv_sem, own_sem,
):
    x, y, z, core = place()
    m = lax.axis_index("mode")
    s = lax.axis_index("slab")
    t = s % 4
    q = block_of(y, z, core)
    number = m * 16 + s

    def peer(off, sign):
        dz, dy, dc = off % 4, (off // 4) % 4, off // 16
        return (y + sign * dy + 4) % 4, (z + sign * dz + 4) % 4, (core + dc) % 2

    def home(index):
        return (index,) + owner_of(4 * m + s // 4)

    def number_of(place_):
        ids = device(*place_)
        return ids[0] * 16 + ids[1]

    def source(part):
        return (q // 4, (q % 4) * 4 + part)

    up, down = q + 1, q - 1
    neighbours = (
        (x > 0, (x - 1, y, z, core)),
        (x < 3, (x + 1, y, z, core)),
        (q > 0, (x,) + owner_of((q + 31) % 32)),
        (q < 31, (x,) + owner_of((q + 1) % 32)),
    )

    barrier = pltpu.get_barrier_semaphore()

    def greet(off, _):
        pl.semaphore_signal(
            barrier, inc=1, device_id=device(x, *peer(off, 1)), device_id_type=MESH
        )
        return 0

    lax.fori_loop(1, 32, greet, 0)
    count = 31
    for inside, other in neighbours[:2]:

        @pl.when(inside)
        def _():
            pl.semaphore_signal(barrier, inc=1, device_id=device(*other), device_id_type=MESH)

        count = count + inside.astype(jnp.int32)
    for index in range(4):
        target = home(index)
        other = number_of(target) != number

        @pl.when(other)
        def _():
            pl.semaphore_signal(barrier, inc=1, device_id=device(*target), device_id_type=MESH)

        origin = source(index)
        foreign = origin[0] * 16 + origin[1] != number

        @pl.when(foreign)
        def _():
            pl.semaphore_signal(barrier, inc=1, device_id=origin, device_id_type=MESH)

        count = count + other.astype(jnp.int32) + foreign.astype(jnp.int32)
    pl.semaphore_wait(barrier, count)

    def copy_out(off):
        py, pz, pc = peer(off, 1)
        rows = pl.multiple_of(8 * block_of(py, pz, pc), 8)
        return pltpu.make_async_remote_copy(
            src_ref=modes.at[:, :, :, pl.ds(rows, 8), :],
            dst_ref=recv.at[m, t],
            send_sem=send_sem.at[off],
            recv_sem=recv_sem.at[off],
            device_id=device(x, py, pz, pc),
            device_id_type=MESH,
        )

    def copy_in(off):
        py, pz, pc = peer(off, -1)
        slot = recv.at[pz * 2 + py // 2, (py % 2) * 2 + pc]
        return pltpu.make_async_remote_copy(
            src_ref=slot,
            dst_ref=slot,
            send_sem=send_sem.at[off],
            recv_sem=recv_sem.at[off],
            device_id=device(x, py, pz, pc),
            device_id_type=MESH,
        )

    def start_out(off, _):
        copy_out(off).start()
        return 0

    lax.fori_loop(1, 32, start_out, 0)
    own_rows = pl.multiple_of(8 * q, 8)
    own = pltpu.make_async_copy(
        modes.at[:, :, :, pl.ds(own_rows, 8), :], recv.at[m, t], own_sem.at[0]
    )
    own.start()

    def volume_out(index):
        return pltpu.make_async_remote_copy(
            src_ref=volume.at[pl.ds(8 * index, 8)],
            dst_ref=vrecv.at[t],
            send_sem=vsend_sem.at[index],
            recv_sem=vrecv_sem.at[t],
            device_id=device(*home(index)),
            device_id_type=MESH,
        )

    def volume_own():
        return pltpu.make_async_copy(volume.at[pl.ds(8 * x, 8)], vrecv.at[t], own_sem.at[1])

    def volume_in(part):
        return pltpu.make_async_remote_copy(
            src_ref=vrecv.at[part],
            dst_ref=vrecv.at[part],
            send_sem=vsend_sem.at[0],
            recv_sem=vrecv_sem.at[part],
            device_id=source(part),
            device_id_type=MESH,
        )

    own_volume = number_of(home(x)) == number
    for index in range(4):
        other = number_of(home(index)) != number

        @pl.when(other)
        def _():
            volume_out(index).start()

    @pl.when(own_volume)
    def _():
        volume_own().start()

    def wait_in(off, _):
        copy_in(off).wait_recv()
        return 0

    lax.fori_loop(1, 32, wait_in, 0)
    own.wait()

    def turn(n, _):
        a = n // 8
        plane = n % 8
        wide[...] = recv[:, plane // 2, :, a, plane % 2].astype(f32).reshape(384, 128)
        for row in range(8):
            uc[a, plane + 2, row + 2] = wide[pl.ds(row, 48, stride=8), :].astype(bf16)
        return 0

    lax.fori_loop(0, 24, turn, 0)

    sent = (
        uc.at[:, 2:4, 2:10],
        uc.at[:, 8:10, 2:10],
        uc.at[:, 2:10, 2:4],
        uc.at[:, 2:10, 8:10],
    )
    landed = (
        uc.at[:, 10:12, 2:10],
        uc.at[:, 0:2, 2:10],
        uc.at[:, 2:10, 10:12],
        uc.at[:, 2:10, 0:2],
    )
    came_to = (1, 0, 3, 2)

    def halo_out(side):
        return pltpu.make_async_remote_copy(
            src_ref=sent[side],
            dst_ref=landed[side],
            send_sem=hsend_sem.at[side],
            recv_sem=hrecv_sem.at[side],
            device_id=device(*neighbours[side][1]),
            device_id_type=MESH,
        )

    for side in (2, 3, 0, 1):

        @pl.when(neighbours[side][0])
        def _():
            halo_out(side).start()

    for side in range(4):
        edge = landed[came_to[side]]

        @pl.when(jnp.logical_not(neighbours[side][0]))
        def _():
            edge[...] = jnp.zeros(edge.shape, bf16)

    def wait_out(off, _):
        copy_out(off).wait_send()
        return 0

    lax.fori_loop(1, 32, wait_out, 0)
    for index in range(4):
        other = number_of(home(index)) != number

        @pl.when(other)
        def _():
            volume_out(index).wait_send()

        origin = source(index)
        foreign = origin[0] * 16 + origin[1] != number

        @pl.when(foreign)
        def _():
            volume_in(index).wait_recv()

    @pl.when(own_volume)
    def _():
        volume_own().wait()

    conv[...] = jnp.zeros_like(conv)
    diss[...] = jnp.zeros_like(diss)

    def tile(xx, pair):
        for r in range(2):
            weight = vrecv[pair, xx, r, :].reshape(1, 128)
            lanes = slice(r * 128, r * 128 + 128)
            for a in range(3):

                def at(dx, dy):
                    return uc[a, xx + 2 + dx, 2 * pair + r + 2 + dy].astype(f32)

                def slope(m2, m1, p1, p2):
                    return (m2 - 8.0 * m1 + 8.0 * p1 - p2) / 12.0

                centre = at(0, 0)
                uv[a, :, lanes] = centre * weight
                slopes = (
                    slope(at(-2, 0), at(-1, 0), at(1, 0), at(2, 0)),
                    slope(at(0, -2), at(0, -1), at(0, 1), at(0, 2)),
                    slope(
                        pltpu.roll(centre, 2, 1),
                        pltpu.roll(centre, 1, 1),
                        pltpu.roll(centre, 127, 1),
                        pltpu.roll(centre, 126, 1),
                    ),
                )
                for b in range(3):
                    rounded = slopes[b].astype(bf16)
                    g[a, b, :, lanes] = rounded
                    gw[a, b * 48 : b * 48 + 48, lanes] = (rounded.astype(f32) * weight).astype(
                        bf16
                    )
        for a in range(3):
            diss[...] += lax.dot_general(
                g[a].reshape(144, 256), gw[a], NT, preferred_element_type=f32
            )
        right = jnp.concatenate(
            [
                jnp.concatenate([uc[b, xx + 2, 2 * pair + 2], uc[b, xx + 2, 2 * pair + 3]], axis=1)
                for b in range(3)
            ],
            axis=1,
        )
        for first in range(0, 48, GROUP):
            rows = []
            for i in range(first, first + GROUP):
                spread = [
                    jnp.broadcast_to(uv[a, pl.ds(i, 1), :], (16, 256)).astype(bf16)
                    for a in range(3)
                ]
                outs = []
                for b in range(3):
                    parts = []
                    for k in range(0, 48, 16):
                        parts.append(
                            spread[0] * g[0, b, k : k + 16, :]
                            + spread[1] * g[1, b, k : k + 16, :]
                            + spread[2] * g[2, b, k : k + 16, :]
                        )
                    outs.append(jnp.concatenate(parts, axis=0))
                rows.append(jnp.concatenate(outs, axis=1))
            conv[first * 48 : (first + GROUP) * 48, :] += lax.dot_general(
                jnp.concatenate(rows, axis=0), right, NT, preferred_element_type=f32
            )

    def halo_in(side):
        pltpu.make_async_remote_copy(
            src_ref=landed[came_to[side]],
            dst_ref=landed[came_to[side]],
            send_sem=hsend_sem.at[came_to[side]],
            recv_sem=hrecv_sem.at[came_to[side]],
            device_id=device(*neighbours[side][1]),
            device_id_type=MESH,
        ).wait_recv()

    def step(n, _):
        edge_x = n // 16
        spot = n % 16
        xx = jnp.where(edge_x == 1, (spot // 4) + 4 * (spot // 8), 2 + spot % 4)
        inner = (spot // 4) % 4
        pair = jnp.where(
            edge_x == 1, spot % 4, jnp.where(inner < 2, 1 + inner, 3 * (inner - 2))
        )

        @pl.when(n == 8)
        def _():
            for side in (2, 3):

                @pl.when(neighbours[side][0])
                def _():
                    halo_in(side)

        @pl.when(n == 16)
        def _():
            for side in (0, 1):

                @pl.when(neighbours[side][0])
                def _():
                    halo_in(side)

        tile(xx, pair)
        return 0

    lax.fori_loop(0, 32, step, 0)
    for side in range(4):

        @pl.when(neighbours[side][0])
        def _():
            halo_out(side).wait_send()


def project(modes, volume):
    whole = pl.BlockSpec(memory_space=pltpu.VMEM)
    apart = pl.BlockSpec(memory_space=pl.ANY)
    return pl.pallas_call(
        main_kernel,
        out_shape=(
            jax.ShapeDtypeStruct((2304, 48), f32),
            jax.ShapeDtypeStruct((144, 144), f32),
        ),
        in_specs=[apart, apart],
        out_specs=(whole, whole),
        scratch_shapes=[
            pltpu.VMEM((8, 4, 6, 3, 2, 8, 128), bf16),
            pltpu.VMEM((4, 8, 2, 128), f32),
            pltpu.VMEM((3, 12, 12, 48, 128), bf16),
            pltpu.VMEM((384, 128), f32),
            pltpu.VMEM((3, 3, 48, 256), bf16),
            pltpu.VMEM((3, 144, 256), bf16),
            pltpu.VMEM((3, 48, 256), f32),
            pltpu.SemaphoreType.DMA((32,)),
            pltpu.SemaphoreType.DMA((32,)),
            pltpu.SemaphoreType.DMA((4,)),
            pltpu.SemaphoreType.DMA((4,)),
            pltpu.SemaphoreType.DMA((4,)),
            pltpu.SemaphoreType.DMA((4,)),
            pltpu.SemaphoreType.DMA((2,)),
        ],
        compiler_params=pltpu.CompilerParams(
            collective_id=0, has_side_effects=True, vmem_limit_bytes=56 << 20
        ),
    )(modes, volume)


def reduce_kernel(
    scales, conv, diss, conv_out, diss_out, dense, pieces, rbuf, dsend, drecv,
    send_sem, recv_sem, dsend_sem, drecv_sem,
):
    x, y, z, core = place()
    me = lax.axis_index("mode") * 16 + lax.axis_index("slab")

    def ids(number):
        return (number // 16, number % 16)

    barrier = pltpu.get_barrier_semaphore()

    def greet(off, _):
        pl.semaphore_signal(
            barrier, inc=1, device_id=ids((me + off) % 128), device_id_type=MESH
        )
        return 0

    lax.fori_loop(1, 128, greet, 0)

    for i in range(24):
        left = jnp.transpose(conv[i * 48 : i * 48 + 48, :])
        right = jnp.transpose(conv[(i + 24) * 48 : (i + 24) * 48 + 48, :])
        dense[i * 48 : i * 48 + 48, :] = jnp.concatenate(
            [left, right, jnp.zeros((48, 32), f32)], axis=1
        )
    dense[1152:, :] = jnp.zeros((8, 128), f32)
    for n in range(64):
        pieces[n] = dense[18 * n : 18 * n + 24, :]
    pl.semaphore_wait(barrier, 127)

    def piece_out(off):
        target = (me + off) % 128
        return pltpu.make_async_remote_copy(
            src_ref=pieces.at[target % 64],
            dst_ref=rbuf.at[me],
            send_sem=send_sem.at[off],
            recv_sem=recv_sem.at[off],
            device_id=ids(target),
            device_id_type=MESH,
        )

    def piece_in(off):
        origin = (me + 128 - off) % 128
        return pltpu.make_async_remote_copy(
            src_ref=rbuf.at[origin],
            dst_ref=rbuf.at[origin],
            send_sem=send_sem.at[off],
            recv_sem=recv_sem.at[off],
            device_id=ids(origin),
            device_id_type=MESH,
        )

    def start_piece(off, _):
        piece_out(off).start()
        return 0

    lax.fori_loop(1, 128, start_piece, 0)

    total = diss[0:48, 0:48] + diss[48:96, 48:96] + diss[96:144, 96:144]
    here = (x, y, z, core)
    for phase, (axis, size) in enumerate(((3, 2), (0, 4), (1, 4), (2, 4))):
        dsend[phase] = total
        at = here[axis]
        copies = []
        for off in range(1, size):
            there = list(here)
            there[axis] = (at + off) % size
            copies.append(
                pltpu.make_async_remote_copy(
                    src_ref=dsend.at[phase],
                    dst_ref=drecv.at[phase, at],
                    send_sem=dsend_sem.at[phase, off],
                    recv_sem=drecv_sem.at[phase, off],
                    device_id=device(*there),
                    device_id_type=MESH,
                )
            )
        for copy in copies:
            copy.start()
        drecv[phase, at] = total
        for off in range(1, size):
            there = list(here)
            there[axis] = (at + size - off) % size
            slot = drecv.at[phase, (at + size - off) % size]
            pltpu.make_async_remote_copy(
                src_ref=slot,
                dst_ref=slot,
                send_sem=dsend_sem.at[phase, off],
                recv_sem=drecv_sem.at[phase, off],
                device_id=device(*there),
                device_id_type=MESH,
            ).wait_recv()
        for copy in copies:
            copy.wait_send()
        total = drecv[phase, 0]
        for other in range(1, size):
            total = total + drecv[phase, other]
    diss_out[...] = total * scales[1]

    rbuf[me] = pieces[me % 64]

    def wait_piece(off, _):
        piece_in(off).wait_recv()
        return 0

    lax.fori_loop(1, 128, wait_piece, 0)

    def gather(n, running):
        return running + rbuf[n]

    summed = lax.fori_loop(0, 128, gather, jnp.zeros((24, 128), f32)) * scales[0]
    shifted = pltpu.roll(summed, 80, 1)

    @pl.when(me < 64)
    def _():
        conv_out[...] = summed[:18, :48]

    @pl.when(me >= 64)
    def _():
        conv_out[...] = shifted[:18, :48]

    def wait_sent(off, _):
        piece_out(off).wait_send()
        return 0

    lax.fori_loop(1, 128, wait_sent, 0)


def scatter(scales, conv, diss):
    whole = pl.BlockSpec(memory_space=pltpu.VMEM)
    return pl.pallas_call(
        lambda *refs: reduce_kernel(scales, *refs),
        out_shape=(
            jax.ShapeDtypeStruct((18, 48), f32),
            jax.ShapeDtypeStruct((48, 48), f32),
        ),
        in_specs=[whole, whole],
        out_specs=(whole, whole),
        scratch_shapes=[
            pltpu.VMEM((1160, 128), f32),
            pltpu.VMEM((64, 24, 128), f32),
            pltpu.VMEM((128, 24, 128), f32),
            pltpu.VMEM((4, 48, 48), f32),
            pltpu.VMEM((4, 4, 48, 48), f32),
            pltpu.SemaphoreType.DMA((128,)),
            pltpu.SemaphoreType.DMA((128,)),
            pltpu.SemaphoreType.DMA((4, 4)),
            pltpu.SemaphoreType.DMA((4, 4)),
        ],
        compiler_params=pltpu.CompilerParams(
            collective_id=1, has_side_effects=True, vmem_limit_bytes=32 << 20
        ),
        name="scatter",
    )(conv, diss)


def per_device(modes, volume):
    cell_total = 32 * 256 * 128
    conv_part, diss_part = project(modes, volume)
    scales = (1.0 / math.sqrt(cell_total), viscosity / cell_total)
    return scatter(scales, conv_part, diss_part)


def solution(mesh):
    placed = (P("mode", None, "slab", None, None), P(None, ("mode", "slab"), None))
    return jax.shard_map(
        per_device,
        mesh=mesh,
        in_specs=placed,
        out_specs=(P(("mode", "slab"), None), P()),
        check_vma=False,
    )
```

```python
import math

import jax
import jax.numpy as jnp
from jax import lax
from jax.experimental import pallas as pl
from jax.experimental.pallas import tpu as pltpu
from jax.sharding import PartitionSpec as P

viscosity = 0.05
bf16 = jnp.bfloat16
f32 = jnp.float32
MESH = pl.DeviceIdType.MESH
NT = (((1,), (1,)), ((), ()))
GROUP = 24
CHUNKS = 4
ROWS = 8 // CHUNKS


def place():
    m = lax.axis_index("mode")
    s = lax.axis_index("slab")
    return s // 4, (m % 2) * 2 + (s % 4) // 2, m // 2, s % 2


def device(x, y, z, core):
    return (z * 2 + y // 2, x * 4 + (y % 2) * 2 + core)


def block_of(y, z, core):
    return 2 * (y * 4 + z + (y % 2) * (3 - 2 * z)) + core


def owner_of(q):
    step = q // 2
    y = step // 4
    along = step % 4
    return y, along + (y % 2) * (3 - 2 * along), q % 2


def unit(b, column, pair, uc, uv, vrecv, g, gw, conv, diss):
    lines = [(2 * column + plane, 2 * pair + row) for plane in range(2) for row in range(2)]
    for n, (plane, row) in enumerate(lines):
        weight = vrecv[pair, plane, n % 2, :].reshape(1, 128)
        lanes = slice(n * 128, n * 128 + 128)
        for a in range(3):

            def at(shift):
                dx, dy = (shift, 0) if b == 0 else (0, shift)
                return uc[a, plane + 2 + dx, row + 2 + dy].astype(f32)

            if b == 2:
                centre = at(0)
                m2, m1, p1, p2 = (pltpu.roll(centre, by, 1) for by in (2, 1, 127, 126))
            else:
                m2, m1, p1, p2 = at(-2), at(-1), at(1), at(2)
            slope = ((m2 - p2) + 8.0 * (p1 - m1)) / 12.0
            rounded = slope.astype(bf16)
            g[a, :, lanes] = rounded
            gw[a * 48 : a * 48 + 48, lanes] = (rounded.astype(f32) * weight).astype(bf16)
    diss[...] += lax.dot_general(g[...].reshape(144, 512), gw[...], NT, preferred_element_type=f32)
    right = jnp.concatenate([uc[b, plane + 2, row + 2] for plane, row in lines], axis=1)
    for first in range(0, 48, GROUP):
        rows = []
        for i in range(first, first + GROUP):
            spread = [
                jnp.concatenate(
                    [
                        jnp.broadcast_to(uv[a, plane, row, pl.ds(i, 1), :], (16, 128)).astype(bf16)
                        for plane, row in lines
                    ],
                    axis=1,
                )
                for a in range(3)
            ]
            parts = [
                spread[0] * g[0, k : k + 16, :]
                + spread[1] * g[1, k : k + 16, :]
                + spread[2] * g[2, k : k + 16, :]
                for k in range(0, 48, 16)
            ]
            rows.append(jnp.concatenate(parts, axis=0))
        conv[first * 48 : (first + GROUP) * 48, :] += lax.dot_general(
            jnp.concatenate(rows, axis=0), right, NT, preferred_element_type=f32
        )


def main_kernel(
    modes, volume, conv, diss, recv, vrecv, uc, uv, wide, g, gw,
    send_sem, recv_sem, vsend_sem, vrecv_sem, xsend_sem, xrecv_sem, ysend_sem, yrecv_sem, own_sem,
):
    x, y, z, core = place()
    m = lax.axis_index("mode")
    s = lax.axis_index("slab")
    t = s % 4
    q = block_of(y, z, core)
    number = m * 16 + s

    def peer(off, sign):
        dz, dy, dc = off % 4, (off // 4) % 4, off // 16
        return (y + sign * dy + 4) % 4, (z + sign * dz + 4) % 4, (core + dc) % 2

    def home(index):
        return (index,) + owner_of(4 * m + s // 4)

    def number_of(place_):
        ids = device(*place_)
        return ids[0] * 16 + ids[1]

    def source(part):
        return (q // 4, (q % 4) * 4 + part)

    neighbours = (
        (x > 0, (x - 1, y, z, core)),
        (x < 3, (x + 1, y, z, core)),
        (q > 0, (x,) + owner_of((q + 31) % 32)),
        (q < 31, (x,) + owner_of((q + 1) % 32)),
    )

    barrier = pltpu.get_barrier_semaphore()

    def greet(off, _):
        pl.semaphore_signal(
            barrier, inc=1, device_id=device(x, *peer(off, 1)), device_id_type=MESH
        )
        return 0

    lax.fori_loop(1, 32, greet, 0)
    count = 31
    for inside, other in neighbours[:2]:

        @pl.when(inside)
        def _():
            pl.semaphore_signal(barrier, inc=1, device_id=device(*other), device_id_type=MESH)

        count = count + inside.astype(jnp.int32)
    for index in range(4):
        target = home(index)
        other = number_of(target) != number

        @pl.when(other)
        def _():
            pl.semaphore_signal(barrier, inc=1, device_id=device(*target), device_id_type=MESH)

        origin = source(index)
        foreign = origin[0] * 16 + origin[1] != number

        @pl.when(foreign)
        def _():
            pl.semaphore_signal(barrier, inc=1, device_id=origin, device_id_type=MESH)

        count = count + other.astype(jnp.int32) + foreign.astype(jnp.int32)
    own_volume = number_of(home(x)) == number

    def volume_out(index):
        return pltpu.make_async_remote_copy(
            src_ref=volume.at[pl.ds(8 * index, 8)],
            dst_ref=vrecv.at[t],
            send_sem=vsend_sem.at[index],
            recv_sem=vrecv_sem.at[t],
            device_id=device(*home(index)),
            device_id_type=MESH,
        )

    def volume_own():
        return pltpu.make_async_copy(volume.at[pl.ds(8 * x, 8)], vrecv.at[t], own_sem.at[CHUNKS])

    def volume_in(part):
        return pltpu.make_async_remote_copy(
            src_ref=vrecv.at[part],
            dst_ref=vrecv.at[part],
            send_sem=vsend_sem.at[0],
            recv_sem=vrecv_sem.at[part],
            device_id=source(part),
            device_id_type=MESH,
        )

    def copy_out(chunk, off):
        py, pz, pc = peer(off, 1)
        first = pl.multiple_of(8 * block_of(py, pz, pc) + ROWS * chunk, ROWS)
        return pltpu.make_async_remote_copy(
            src_ref=modes.at[:, :, :, pl.ds(first, ROWS), :],
            dst_ref=recv.at[chunk, m, t],
            send_sem=send_sem.at[chunk, off],
            recv_sem=recv_sem.at[chunk, off],
            device_id=device(x, py, pz, pc),
            device_id_type=MESH,
        )

    def copy_in(chunk, off):
        py, pz, pc = peer(off, -1)
        slot = recv.at[chunk, pz * 2 + py // 2, (py % 2) * 2 + pc]
        return pltpu.make_async_remote_copy(
            src_ref=slot,
            dst_ref=slot,
            send_sem=send_sem.at[chunk, off],
            recv_sem=recv_sem.at[chunk, off],
            device_id=device(x, py, pz, pc),
            device_id_type=MESH,
        )

    def copy_own(chunk):
        first = pl.multiple_of(8 * q + ROWS * chunk, ROWS)
        return pltpu.make_async_copy(
            modes.at[:, :, :, pl.ds(first, ROWS), :], recv.at[chunk, m, t], own_sem.at[chunk]
        )

    @pl.when(own_volume)
    def _():
        volume_own().start()

    for chunk in range(CHUNKS):
        copy_own(chunk).start()

    edges = (uc.at[:, 0:2, 2:10], uc.at[:, 10:12, 2:10], uc.at[:, 2:10, 0:2], uc.at[:, 2:10, 10:12])
    for side in range(4):

        @pl.when(jnp.logical_not(neighbours[side][0]))
        def _():
            edges[side][...] = jnp.zeros(edges[side].shape, bf16)

    conv[...] = jnp.zeros_like(conv)
    diss[...] = jnp.zeros_like(diss)
    pl.semaphore_wait(barrier, count)

    for index in range(4):
        other = number_of(home(index)) != number

        @pl.when(other)
        def _():
            volume_out(index).start()

    def start_out(n, _):
        copy_out(n // 31, n % 31 + 1).start()
        return 0

    lax.fori_loop(0, 31 * CHUNKS, start_out, 0)

    for index in range(4):
        origin = source(index)
        foreign = origin[0] * 16 + origin[1] != number

        @pl.when(foreign)
        def _():
            volume_in(index).wait_recv()

    @pl.when(own_volume)
    def _():
        volume_own().wait()

    def x_copy(side, chunk):
        rows = pl.ds(2 + ROWS * chunk, ROWS)
        planes, there = ((2, 10), (8, 0))[side]
        return pltpu.make_async_remote_copy(
            src_ref=uc.at[:, planes : planes + 2, rows],
            dst_ref=uc.at[:, there : there + 2, rows],
            send_sem=xsend_sem.at[side, chunk],
            recv_sem=xrecv_sem.at[side, chunk],
            device_id=device(*neighbours[side][1]),
            device_id_type=MESH,
        )

    def x_arrival(side, chunk):
        rows = pl.ds(2 + ROWS * chunk, ROWS)
        there = (0, 10)[side]
        return pltpu.make_async_remote_copy(
            src_ref=uc.at[:, there : there + 2, rows],
            dst_ref=uc.at[:, there : there + 2, rows],
            send_sem=xsend_sem.at[1 - side, chunk],
            recv_sem=xrecv_sem.at[1 - side, chunk],
            device_id=device(*neighbours[side][1]),
            device_id_type=MESH,
        )

    def y_copy(side):
        rows, there = ((2, 10), (8, 0))[side]
        return pltpu.make_async_remote_copy(
            src_ref=uc.at[:, 2:10, rows : rows + 2],
            dst_ref=uc.at[:, 2:10, there : there + 2],
            send_sem=ysend_sem.at[side],
            recv_sem=yrecv_sem.at[side],
            device_id=device(*neighbours[2 + side][1]),
            device_id_type=MESH,
        )

    def y_arrival(side):
        there = (0, 10)[side]
        return pltpu.make_async_remote_copy(
            src_ref=uc.at[:, 2:10, there : there + 2],
            dst_ref=uc.at[:, 2:10, there : there + 2],
            send_sem=ysend_sem.at[1 - side],
            recv_sem=yrecv_sem.at[1 - side],
            device_id=device(*neighbours[2 + side][1]),
            device_id_type=MESH,
        )

    def work(b, column, pair):
        unit(b, column, pair, uc, uv, vrecv, g, gw, conv, diss)

    def arrive(chunk, _):
        def wait_in(off, _):
            copy_in(chunk, off).wait_recv()
            return 0

        lax.fori_loop(1, 32, wait_in, 0)
        copy_own(chunk).wait()

        def turn(n, _):
            a = n // 8
            plane = n % 8
            wide[:, 0:ROWS, :] = (
                recv[chunk, :, plane // 2, :, a, plane % 2].astype(f32).reshape(48, ROWS, 128)
            )
            for row in range(ROWS):
                here = ROWS * chunk + row
                field = wide.reshape(384, 128)[pl.ds(row, 48, stride=8), :]
                uc[a, plane + 2, here + 2] = field.astype(bf16)
                weight = vrecv[here // 2, plane, pl.ds(here % 2, 1), :].reshape(1, 128)
                uv[a, plane, here] = field * weight
            return 0

        lax.fori_loop(0, 24, turn, 0)

        for side in range(2):

            @pl.when(neighbours[side][0])
            def _():
                x_copy(side, chunk).start()

        @pl.when(jnp.logical_and(chunk == 0, neighbours[2][0]))
        def _():
            y_copy(0).start()

        @pl.when(jnp.logical_and(chunk == CHUNKS - 1, neighbours[3][0]))
        def _():
            y_copy(1).start()

        def along_z(n, _):
            work(2, n % 4, chunk * (ROWS // 2) + n // 4)
            return 0

        lax.fori_loop(0, 2 * ROWS, along_z, 0)

        def along_x(n, _):
            work(0, 1 + n % 2, chunk * (ROWS // 2) + n // 2)
            return 0

        lax.fori_loop(0, ROWS, along_x, 0)
        return 0

    lax.fori_loop(0, CHUNKS, arrive, 0)

    for side in range(2):
        for chunk in range(CHUNKS):

            @pl.when(neighbours[side][0])
            def _():
                x_arrival(side, chunk).wait_recv()

    def along_x_edge(n, _):
        work(0, 3 * (n % 2), n // 2)
        return 0

    lax.fori_loop(0, 8, along_x_edge, 0)

    def along_y(n, _):
        @pl.when(n == 8)
        def _():
            for side in range(2):

                @pl.when(neighbours[2 + side][0])
                def _():
                    y_arrival(side).wait_recv()

        half = (n // 4) % 2
        work(1, n % 4, jnp.where(n < 8, 1 + half, 3 * half))
        return 0

    lax.fori_loop(0, 16, along_y, 0)

    def wait_out(n, _):
        copy_out(n // 31, n % 31 + 1).wait_send()
        return 0

    lax.fori_loop(0, 31 * CHUNKS, wait_out, 0)
    for index in range(4):
        other = number_of(home(index)) != number

        @pl.when(other)
        def _():
            volume_out(index).wait_send()

    for side in range(2):

        @pl.when(neighbours[side][0])
        def _():
            for chunk in range(CHUNKS):
                x_copy(side, chunk).wait_send()

        @pl.when(neighbours[2 + side][0])
        def _():
            y_copy(side).wait_send()


def project(modes, volume):
    whole = pl.BlockSpec(memory_space=pltpu.VMEM)
    apart = pl.BlockSpec(memory_space=pl.ANY)
    return pl.pallas_call(
        main_kernel,
        out_shape=(
            jax.ShapeDtypeStruct((2304, 48), f32),
            jax.ShapeDtypeStruct((144, 144), f32),
        ),
        in_specs=[apart, apart],
        out_specs=(whole, whole),
        scratch_shapes=[
            pltpu.VMEM((CHUNKS, 8, 4, 6, 3, 2, ROWS, 128), bf16),
            pltpu.VMEM((4, 8, 2, 128), f32),
            pltpu.VMEM((3, 12, 12, 48, 128), bf16),
            pltpu.VMEM((3, 8, 8, 48, 128), f32),
            pltpu.VMEM((48, 8, 128), f32),
            pltpu.VMEM((3, 48, 512), bf16),
            pltpu.VMEM((144, 512), bf16),
            pltpu.SemaphoreType.DMA((CHUNKS, 32)),
            pltpu.SemaphoreType.DMA((CHUNKS, 32)),
            pltpu.SemaphoreType.DMA((4,)),
            pltpu.SemaphoreType.DMA((4,)),
            pltpu.SemaphoreType.DMA((2, CHUNKS)),
            pltpu.SemaphoreType.DMA((2, CHUNKS)),
            pltpu.SemaphoreType.DMA((2,)),
            pltpu.SemaphoreType.DMA((2,)),
            pltpu.SemaphoreType.DMA((CHUNKS + 1,)),
        ],
        compiler_params=pltpu.CompilerParams(
            collective_id=0, has_side_effects=True, vmem_limit_bytes=56 << 20
        ),
    )(modes, volume)


def reduce_kernel(
    scales, conv, diss, conv_out, diss_out, turned, pieces, rbuf, dsend, drecv,
    send_sem, recv_sem, dsend_sem, drecv_sem,
):
    x, y, z, core = place()
    me = lax.axis_index("mode") * 16 + lax.axis_index("slab")

    def ids(number):
        return (number // 16, number % 16)

    barrier = pltpu.get_barrier_semaphore()

    def greet(off, _):
        pl.semaphore_signal(
            barrier, inc=1, device_id=ids((me + off) % 128), device_id_type=MESH
        )
        return 0

    lax.fori_loop(1, 128, greet, 0)

    for i in range(48):
        turned[i * 48 : i * 48 + 48, :] = jnp.transpose(conv[i * 48 : i * 48 + 48, :])
    turned[2304:, :] = jnp.zeros((8, 48), f32)
    lane = lax.broadcasted_iota(jnp.int32, (8, 128), 1)
    line = lax.broadcasted_iota(jnp.int32, (8, 128), 0)

    def padded(first):
        return jnp.concatenate([turned[first : first + 8, :], jnp.zeros((8, 80), f32)], axis=1)

    for n in range(128):
        packed = jnp.where(lane < 48, padded(18 * n), pltpu.roll(padded(18 * n + 8), 48, 1))
        for third in range(3):
            ends = pltpu.roll(padded(18 * n + 16 - 2 * third), 96 - 16 * third, 1)
            there = (lane >= 96) & (lane < 112) & (line // 2 == third)
            packed = jnp.where(there, ends, packed)
        pieces[n] = packed
    pl.semaphore_wait(barrier, 127)

    def piece_out(off):
        target = (me + 37 * off) % 128
        return pltpu.make_async_remote_copy(
            src_ref=pieces.at[target],
            dst_ref=rbuf.at[me],
            send_sem=send_sem.at[off],
            recv_sem=recv_sem.at[off],
            device_id=ids(target),
            device_id_type=MESH,
        )

    def piece_in(off):
        origin = (me + 128 - (37 * off) % 128) % 128
        return pltpu.make_async_remote_copy(
            src_ref=rbuf.at[origin],
            dst_ref=rbuf.at[origin],
            send_sem=send_sem.at[off],
            recv_sem=recv_sem.at[off],
            device_id=ids(origin),
            device_id_type=MESH,
        )

    def start_piece(off, _):
        piece_out(off).start()
        return 0

    lax.fori_loop(1, 128, start_piece, 0)

    total = diss[0:48, 0:48] + diss[48:96, 48:96] + diss[96:144, 96:144]
    here = (x, y, z, core)
    for phase, (axis, size) in enumerate(((3, 2), (0, 4), (1, 4), (2, 4))):
        dsend[phase] = total
        at = here[axis]
        copies = []
        for off in range(1, size):
            there = list(here)
            there[axis] = (at + off) % size
            copies.append(
                pltpu.make_async_remote_copy(
                    src_ref=dsend.at[phase],
                    dst_ref=drecv.at[phase, at],
                    send_sem=dsend_sem.at[phase, off],
                    recv_sem=drecv_sem.at[phase, off],
                    device_id=device(*there),
                    device_id_type=MESH,
                )
            )
        for copy in copies:
            copy.start()
        drecv[phase, at] = total
        for off in range(1, size):
            there = list(here)
            there[axis] = (at + size - off) % size
            slot = drecv.at[phase, (at + size - off) % size]
            pltpu.make_async_remote_copy(
                src_ref=slot,
                dst_ref=slot,
                send_sem=dsend_sem.at[phase, off],
                recv_sem=drecv_sem.at[phase, off],
                device_id=device(*there),
                device_id_type=MESH,
            ).wait_recv()
        for copy in copies:
            copy.wait_send()
        total = drecv[phase, 0]
        for other in range(1, size):
            total = total + drecv[phase, other]
    diss_out[...] = total * scales[1]

    rbuf[me] = pieces[me]

    def wait_piece(off, _):
        piece_in(off).wait_recv()
        return 0

    lax.fori_loop(1, 128, wait_piece, 0)

    def gather(n, running):
        return running + rbuf[n]

    summed = lax.fori_loop(0, 128, gather, jnp.zeros((8, 128), f32)) * scales[0]
    conv_out[0:8, :] = summed[:, :48]
    conv_out[8:16, :] = pltpu.roll(summed, 80, 1)[:, :48]
    ends = jnp.zeros((8, 128), f32)
    for third in range(3):
        piece = pltpu.roll(summed, (128 - 96 + 16 * third) % 128, 1)
        piece = pltpu.roll(piece, (8 - 2 * third) % 8, 0) if third else piece
        ends = jnp.where((lane >= 16 * third) & (lane < 16 * third + 16), piece, ends)
    conv_out[16:18, :] = ends[:2, :48]

    def wait_sent(off, _):
        piece_out(off).wait_send()
        return 0

    lax.fori_loop(1, 128, wait_sent, 0)


def scatter(scales, conv, diss):
    whole = pl.BlockSpec(memory_space=pltpu.VMEM)
    return pl.pallas_call(
        lambda *refs: reduce_kernel(scales, *refs),
        out_shape=(
            jax.ShapeDtypeStruct((18, 48), f32),
            jax.ShapeDtypeStruct((48, 48), f32),
        ),
        in_specs=[whole, whole],
        out_specs=(whole, whole),
        scratch_shapes=[
            pltpu.VMEM((2312, 48), f32),
            pltpu.VMEM((128, 8, 128), f32),
            pltpu.VMEM((128, 8, 128), f32),
            pltpu.VMEM((4, 48, 48), f32),
            pltpu.VMEM((4, 4, 48, 48), f32),
            pltpu.SemaphoreType.DMA((128,)),
            pltpu.SemaphoreType.DMA((128,)),
            pltpu.SemaphoreType.DMA((4, 4)),
            pltpu.SemaphoreType.DMA((4, 4)),
        ],
        compiler_params=pltpu.CompilerParams(
            collective_id=1, has_side_effects=True, vmem_limit_bytes=32 << 20
        ),
        name="scatter",
    )(conv, diss)


def per_device(modes, volume):
    cell_total = 32 * 256 * 128
    conv_part, diss_part = project(modes, volume)
    scales = (1.0 / math.sqrt(cell_total), viscosity / cell_total)
    return scatter(scales, conv_part, diss_part)


def solution(mesh):
    placed = (P("mode", None, "slab", None, None), P(None, ("mode", "slab"), None))
    return jax.shard_map(
        per_device,
        mesh=mesh,
        in_specs=placed,
        out_specs=(P(("mode", "slab"), None), P()),
        check_vma=False,
    )
```

```python
import functools
import math

import jax
import jax.numpy as jnp
from jax import lax
from jax.experimental import pallas as pl
from jax.experimental.pallas import tpu as pltpu
from jax.sharding import PartitionSpec as P

viscosity = 0.05
bf16 = jnp.bfloat16
f32 = jnp.float32
MESH = pl.DeviceIdType.MESH
NT = (((1,), (1,)), ((), ()))
GROUP = 24
CHUNKS = 4
ROWS = 8 // CHUNKS
AXES = ((3, 2), (0, 4), (1, 4), (2, 4))


def place():
    m = lax.axis_index("mode")
    s = lax.axis_index("slab")
    return s // 4, (m % 2) * 2 + (s % 4) // 2, m // 2, s % 2


def device(x, y, z, core):
    return (z * 2 + y // 2, x * 4 + (y % 2) * 2 + core)


def block_of(y, z, core):
    return 2 * (y * 4 + z + (y % 2) * (3 - 2 * z)) + core


def owner_of(q):
    step = q // 2
    y = step // 4
    along = step % 4
    return y, along + (y % 2) * (3 - 2 * along), q % 2


def lines_of(column, pair):
    return [(2 * column + plane, 2 * pair + row) for plane in range(2) for row in range(2)]


def slopes(b, column, pair, uc, vrecv, g, gw):
    for n, (plane, row) in enumerate(lines_of(column, pair)):
        weight = vrecv[pair, plane, n % 2, :].reshape(1, 128)
        lanes = slice(n * 128, n * 128 + 128)
        for a in range(3):

            def at(shift):
                dx, dy = (shift, 0) if b == 0 else (0, shift)
                return uc[a, plane + 2 + dx, row + 2 + dy].astype(f32)

            if b == 2:
                centre = at(0)
                m2, m1, p1, p2 = (pltpu.roll(centre, by, 1) for by in (2, 1, 127, 126))
            else:
                m2, m1, p1, p2 = at(-2), at(-1), at(1), at(2)
            rounded = (((m2 - p2) + 8.0 * (p1 - m1)) * (1.0 / 12.0)).astype(bf16)
            g[a, :, lanes] = rounded
            gw[a * 48 : a * 48 + 48, lanes] = (rounded.astype(f32) * weight).astype(bf16)


def products(modes_i, lines, uv, g):
    rows = []
    for i in modes_i:
        spread = [
            jnp.concatenate(
                [
                    jnp.broadcast_to(uv[a, plane, row, pl.ds(i, 1), :], (16, 128)).astype(bf16)
                    for plane, row in lines
                ],
                axis=1,
            )
            for a in range(3)
        ]
        for k in range(0, 48, 16):
            rows.append(
                spread[0] * g[0, k : k + 16, :]
                + spread[1] * g[1, k : k + 16, :]
                + spread[2] * g[2, k : k + 16, :]
            )
    return jnp.concatenate(rows, axis=0)


def advected(b, lines, uc):
    return jnp.concatenate([uc[b, plane + 2, row + 2] for plane, row in lines], axis=1)


def viscous(g, gw, diss):
    diss[...] += lax.dot_general(g[...].reshape(144, 512), gw[...], NT, preferred_element_type=f32)


def contract(b, column, pair, uc, uv, g, gw, conv, diss):
    lines = lines_of(column, pair)
    right = advected(b, lines, uc)
    for first in range(0, 48, GROUP):
        conv[first * 48 : (first + GROUP) * 48, :] += lax.dot_general(
            products(range(first, first + GROUP), lines, uv, g),
            right,
            NT,
            preferred_element_type=f32,
        )
    viscous(g, gw, diss)


def four_units(b, pair, uc, uv, vrecv, g, gw, conv, diss):
    slopes(b, 0, pair, uc, vrecv, g.at[0], gw.at[0])
    for n in range(4):
        if n < 3:
            slopes(b, n + 1, pair, uc, vrecv, g.at[n + 1], gw.at[n + 1])
        contract(b, n, pair, uc, uv, g.at[n], gw.at[n], conv, diss)


def main_kernel(
    scales, modes, volume, conv_out, diss_out,
    recv, vrecv, uc, uv, wide, g, gw, last_g, conv, diss, turned, pieces, rbuf, dsend, drecv,
    send_sem, recv_sem, vsend_sem, vrecv_sem, xsend_sem, xrecv_sem, ysend_sem, yrecv_sem, own_sem,
    psend_sem, precv_sem, dsend_sem, drecv_sem, ready_sem,
):
    x, y, z, core = place()
    m = lax.axis_index("mode")
    s = lax.axis_index("slab")
    t = s % 4
    q = block_of(y, z, core)
    number = m * 16 + s

    def peer(off, sign):
        dz, dy, dc = off % 4, (off // 4) % 4, off // 16
        return (y + sign * dy + 4) % 4, (z + sign * dz + 4) % 4, (core + dc) % 2

    def home(index):
        return (index,) + owner_of(4 * m + s // 4)

    def number_of(place_):
        ids = device(*place_)
        return ids[0] * 16 + ids[1]

    def source(part):
        return (q // 4, (q % 4) * 4 + part)

    neighbours = (
        (x > 0, (x - 1, y, z, core)),
        (x < 3, (x + 1, y, z, core)),
        (q > 0, (x,) + owner_of((q + 31) % 32)),
        (q < 31, (x,) + owner_of((q + 1) % 32)),
    )

    barrier = pltpu.get_barrier_semaphore()

    def greet(off, _):
        pl.semaphore_signal(
            barrier, inc=1, device_id=device(x, *peer(off, 1)), device_id_type=MESH
        )
        return 0

    lax.fori_loop(1, 32, greet, 0)
    for step in range(1, 4):
        pl.semaphore_signal(
            barrier, inc=1, device_id=device((x + step) % 4, y, z, core), device_id_type=MESH
        )
    count = 34
    for index in range(4):
        target = home(index)
        other = number_of(target) != number

        @pl.when(other)
        def _():
            pl.semaphore_signal(barrier, inc=1, device_id=device(*target), device_id_type=MESH)

        origin = source(index)
        foreign = origin[0] * 16 + origin[1] != number

        @pl.when(foreign)
        def _():
            pl.semaphore_signal(barrier, inc=1, device_id=origin, device_id_type=MESH)

        count = count + other.astype(jnp.int32) + foreign.astype(jnp.int32)
    own_volume = number_of(home(x)) == number

    def volume_out(index):
        return pltpu.make_async_remote_copy(
            src_ref=volume.at[pl.ds(8 * index, 8)],
            dst_ref=vrecv.at[t],
            send_sem=vsend_sem.at[index],
            recv_sem=vrecv_sem.at[t],
            device_id=device(*home(index)),
            device_id_type=MESH,
        )

    def volume_own():
        return pltpu.make_async_copy(volume.at[pl.ds(8 * x, 8)], vrecv.at[t], own_sem.at[CHUNKS])

    def volume_in(part):
        return pltpu.make_async_remote_copy(
            src_ref=vrecv.at[part],
            dst_ref=vrecv.at[part],
            send_sem=vsend_sem.at[0],
            recv_sem=vrecv_sem.at[part],
            device_id=source(part),
            device_id_type=MESH,
        )

    def copy_out(chunk, off):
        py, pz, pc = peer(off, 1)
        first = pl.multiple_of(8 * block_of(py, pz, pc) + ROWS * chunk, ROWS)
        return pltpu.make_async_remote_copy(
            src_ref=modes.at[:, :, :, pl.ds(first, ROWS), :],
            dst_ref=recv.at[chunk, m, t],
            send_sem=send_sem.at[chunk, off],
            recv_sem=recv_sem.at[chunk, off],
            device_id=device(x, py, pz, pc),
            device_id_type=MESH,
        )

    def copy_in(chunk, off):
        py, pz, pc = peer(off, -1)
        slot = recv.at[chunk, pz * 2 + py // 2, (py % 2) * 2 + pc]
        return pltpu.make_async_remote_copy(
            src_ref=slot,
            dst_ref=slot,
            send_sem=send_sem.at[chunk, off],
            recv_sem=recv_sem.at[chunk, off],
            device_id=device(x, py, pz, pc),
            device_id_type=MESH,
        )

    def copy_own(chunk):
        first = pl.multiple_of(8 * q + ROWS * chunk, ROWS)
        return pltpu.make_async_copy(
            modes.at[:, :, :, pl.ds(first, ROWS), :], recv.at[chunk, m, t], own_sem.at[chunk]
        )

    @pl.when(own_volume)
    def _():
        volume_own().start()

    for chunk in range(CHUNKS):
        copy_own(chunk).start()

    edges = (uc.at[:, 0:2, 2:10], uc.at[:, 10:12, 2:10], uc.at[:, 2:10, 0:2], uc.at[:, 2:10, 10:12])
    for side in range(4):

        @pl.when(jnp.logical_not(neighbours[side][0]))
        def _():
            edges[side][...] = jnp.zeros(edges[side].shape, bf16)

    conv[...] = jnp.zeros_like(conv)
    diss[...] = jnp.zeros_like(diss)
    turned[576:, :] = jnp.zeros((8, 48), f32)
    pl.semaphore_wait(barrier, count)
    for step in range(1, 4):
        pl.semaphore_signal(
            ready_sem, inc=1, device_id=device((x + step) % 4, y, z, core), device_id_type=MESH
        )

    for index in range(4):
        other = number_of(home(index)) != number

        @pl.when(other)
        def _():
            volume_out(index).start()

    def start_out(n, _):
        copy_out(n // 31, n % 31 + 1).start()
        return 0

    lax.fori_loop(0, 31 * CHUNKS, start_out, 0)

    for index in range(4):
        origin = source(index)
        foreign = origin[0] * 16 + origin[1] != number

        @pl.when(foreign)
        def _():
            volume_in(index).wait_recv()

    @pl.when(own_volume)
    def _():
        volume_own().wait()

    def x_copy(side, chunk):
        rows = pl.ds(2 + ROWS * chunk, ROWS)
        planes, there = ((2, 10), (8, 0))[side]
        return pltpu.make_async_remote_copy(
            src_ref=uc.at[:, planes : planes + 2, rows],
            dst_ref=uc.at[:, there : there + 2, rows],
            send_sem=xsend_sem.at[side, chunk],
            recv_sem=xrecv_sem.at[side, chunk],
            device_id=device(*neighbours[side][1]),
            device_id_type=MESH,
        )

    def x_arrival(side, chunk):
        rows = pl.ds(2 + ROWS * chunk, ROWS)
        there = (0, 10)[side]
        return pltpu.make_async_remote_copy(
            src_ref=uc.at[:, there : there + 2, rows],
            dst_ref=uc.at[:, there : there + 2, rows],
            send_sem=xsend_sem.at[1 - side, chunk],
            recv_sem=xrecv_sem.at[1 - side, chunk],
            device_id=device(*neighbours[side][1]),
            device_id_type=MESH,
        )

    def y_copy(side):
        rows, there = ((2, 10), (8, 0))[side]
        return pltpu.make_async_remote_copy(
            src_ref=uc.at[:, 2:10, rows : rows + 2],
            dst_ref=uc.at[:, 2:10, there : there + 2],
            send_sem=ysend_sem.at[side],
            recv_sem=yrecv_sem.at[side],
            device_id=device(*neighbours[2 + side][1]),
            device_id_type=MESH,
        )

    def y_arrival(side):
        there = (0, 10)[side]
        return pltpu.make_async_remote_copy(
            src_ref=uc.at[:, 2:10, there : there + 2],
            dst_ref=uc.at[:, 2:10, there : there + 2],
            send_sem=ysend_sem.at[1 - side],
            recv_sem=yrecv_sem.at[1 - side],
            device_id=device(*neighbours[2 + side][1]),
            device_id_type=MESH,
        )

    def arrive(chunk):
        def wait_in(off, _):
            copy_in(chunk, off).wait_recv()
            return 0

        lax.fori_loop(1, 32, wait_in, 0)
        copy_own(chunk).wait()

        def turn(n, _):
            a = n // 8
            plane = n % 8
            wide[:, 0:ROWS, :] = (
                recv[chunk, :, plane // 2, :, a, plane % 2].astype(f32).reshape(48, ROWS, 128)
            )
            for row in range(ROWS):
                here = ROWS * chunk + row
                field = wide.reshape(384, 128)[pl.ds(row, 48, stride=8), :]
                uc[a, plane + 2, here + 2] = field.astype(bf16)
                weight = vrecv[here // 2, plane, pl.ds(here % 2, 1), :].reshape(1, 128)
                uv[a, plane, here] = field * weight
            return 0

        lax.fori_loop(0, 24, turn, 0)

        for side in range(2):

            @pl.when(neighbours[side][0])
            def _():
                x_copy(side, chunk).start()

        @pl.when(jnp.logical_and(chunk == 0, neighbours[2][0]))
        def _():
            y_copy(0).start()

        @pl.when(jnp.logical_and(chunk == CHUNKS - 1, neighbours[3][0]))
        def _():
            y_copy(1).start()

    def work(b, pair):
        four_units(b, pair, uc, uv, vrecv, g, gw, conv, diss)

    def advance(chunk, _):
        @pl.when(chunk < CHUNKS)
        def _():
            arrive(chunk)
            work(2, chunk)

        @pl.when(chunk >= 1)
        def _():
            for side in range(2):

                @pl.when(neighbours[side][0])
                def _():
                    x_arrival(side, chunk - 1).wait_recv()

            work(0, chunk - 1)

        @pl.when(jnp.logical_or(chunk == 2, chunk == 4))
        def _():
            work(1, chunk // 2)

        return 0

    lax.fori_loop(0, CHUNKS + 1, advance, 0)

    for side in range(2):

        @pl.when(neighbours[2 + side][0])
        def _():
            y_arrival(side).wait_recv()

    def last_slopes(half, _):
        for n in range(4):
            slot = last_g.at[4 * half + n]
            slopes(1, n, 3 * half, uc, vrecv, slot, gw.at[n])
            viscous(slot, gw.at[n], diss)
        return 0

    lax.fori_loop(0, 2, last_slopes, 0)

    here = (x, y, z, core)

    def viscous_copy(phase, off, sign):
        axis, size = AXES[phase]
        there = list(here)
        there[axis] = (here[axis] + sign * off + size) % size
        slot = drecv.at[phase, here[axis] if sign > 0 else there[axis]]
        return pltpu.make_async_remote_copy(
            src_ref=dsend.at[phase] if sign > 0 else slot,
            dst_ref=slot,
            send_sem=dsend_sem.at[phase, off],
            recv_sem=drecv_sem.at[phase, off],
            device_id=device(*there),
            device_id_type=MESH,
        )

    def viscous_start(phase, total):
        dsend[phase] = total
        drecv[phase, here[AXES[phase][0]]] = total
        for off in range(1, AXES[phase][1]):
            viscous_copy(phase, off, 1).start()

    def viscous_end(phase):
        size = AXES[phase][1]
        for off in range(1, size):
            viscous_copy(phase, off, -1).wait_recv()
        total = drecv[phase, 0]
        for other in range(1, size):
            total = total + drecv[phase, other]
        return total

    viscous_start(0, diss[0:48, 0:48] + diss[48:96, 48:96] + diss[96:144, 96:144])
    pl.semaphore_wait(ready_sem, 3)

    me = number
    lane = lax.broadcasted_iota(jnp.int32, (8, 128), 1)
    line = lax.broadcasted_iota(jnp.int32, (8, 128), 0)

    def padded(first):
        return jnp.concatenate([turned[first : first + 8, :], jnp.zeros((8, 80), f32)], axis=1)

    def packed(first):
        tile = jnp.where(lane < 48, padded(first), pltpu.roll(padded(first + 8), 48, 1))
        for third in range(3):
            ends = pltpu.roll(padded(first + 16 - 2 * third), 96 - 16 * third, 1)
            tile = jnp.where((lane >= 96) & (lane < 112) & (line // 2 == third), ends, tile)
        return tile

    def piece_out(target):
        return pltpu.make_async_remote_copy(
            src_ref=pieces.at[target],
            dst_ref=rbuf.at[me],
            send_sem=psend_sem.at[target],
            recv_sem=precv_sem.at[me],
            device_id=(target // 16, target % 16),
            device_id_type=MESH,
        )

    def piece_in(origin):
        return pltpu.make_async_remote_copy(
            src_ref=rbuf.at[origin],
            dst_ref=rbuf.at[origin],
            send_sem=psend_sem.at[origin],
            recv_sem=precv_sem.at[origin],
            device_id=(origin // 16, origin % 16),
            device_id_type=MESH,
        )

    def triple_of(part, number_):
        return 4 * part + (part + number_) % 4

    def finish(number_, _):
        modes_i = [3 * triple_of(part, number_) + e for part in range(4) for e in range(3)]
        for n in range(8):
            lines = lines_of(n % 4, 3 * (n // 4))
            sums = lax.dot_general(
                products(modes_i, lines, uv, last_g.at[n]),
                advected(1, lines, uc),
                NT,
                preferred_element_type=f32,
            )
            for part in range(4):
                first = pl.multiple_of(144 * triple_of(part, number_), 8)
                conv[pl.ds(first, 144), :] += sums[part * 144 : part * 144 + 144]
        for phase in range(4):

            @pl.when(number_ == phase)
            def _():
                total = viscous_end(phase)
                if phase < 3:
                    viscous_start(phase + 1, total)
                else:
                    diss_out[...] = total * scales[1]

        for part in range(4):
            for e in range(3):
                first = pl.multiple_of(144 * triple_of(part, number_) + 48 * e, 8)
                turned[part * 144 + e * 48 : part * 144 + e * 48 + 48, :] = jnp.transpose(
                    conv[pl.ds(first, 48), :]
                )
        for part in range(4):
            for r in range(8):
                pieces[8 * triple_of(part, number_) + r] = packed(part * 144 + 18 * r)

        def send(n, _):
            target = 8 * triple_of((z + n) % 4, number_) + (me + n // 4) % 8

            @pl.when(target != me)
            def _():
                piece_out(target).start()

            @pl.when(target == me)
            def _():
                rbuf[me] = pieces[me]

            return 0

        lax.fori_loop(0, 32, send, 0)
        return 0

    lax.fori_loop(0, 4, finish, 0)

    def wait_piece(origin, _):
        @pl.when(origin != me)
        def _():
            piece_in(origin).wait_recv()

        return 0

    lax.fori_loop(0, 128, wait_piece, 0)

    def gather(n, running):
        return running + rbuf[n]

    summed = lax.fori_loop(0, 128, gather, jnp.zeros((8, 128), f32)) * scales[0]
    conv_out[0:8, :] = summed[:, :48]
    conv_out[8:16, :] = pltpu.roll(summed, 80, 1)[:, :48]
    ends = jnp.zeros((8, 128), f32)
    for third in range(3):
        piece = pltpu.roll(summed, 32 + 16 * third, 1)
        piece = pltpu.roll(piece, 8 - 2 * third, 0) if third else piece
        ends = jnp.where((lane >= 16 * third) & (lane < 16 * third + 16), piece, ends)
    conv_out[16:18, :] = ends[:2, :48]

    def wait_out(n, _):
        copy_out(n // 31, n % 31 + 1).wait_send()
        return 0

    lax.fori_loop(0, 31 * CHUNKS, wait_out, 0)
    for index in range(4):
        other = number_of(home(index)) != number

        @pl.when(other)
        def _():
            volume_out(index).wait_send()

    for side in range(2):

        @pl.when(neighbours[side][0])
        def _():
            for chunk in range(CHUNKS):
                x_copy(side, chunk).wait_send()

        @pl.when(neighbours[2 + side][0])
        def _():
            y_copy(side).wait_send()

    for phase in range(4):
        for off in range(1, AXES[phase][1]):
            viscous_copy(phase, off, 1).wait_send()

    def wait_sent(target, _):
        @pl.when(target != me)
        def _():
            piece_out(target).wait_send()

        return 0

    lax.fori_loop(0, 128, wait_sent, 0)


def per_device(modes, volume):
    cell_total = 32 * 256 * 128
    scales = (1.0 / math.sqrt(cell_total), viscosity / cell_total)
    whole = pl.BlockSpec(memory_space=pltpu.VMEM)
    apart = pl.BlockSpec(memory_space=pl.ANY)
    dma = pltpu.SemaphoreType.DMA
    return pl.pallas_call(
        functools.partial(main_kernel, scales),
        out_shape=(
            jax.ShapeDtypeStruct((18, 48), f32),
            jax.ShapeDtypeStruct((48, 48), f32),
        ),
        in_specs=[apart, apart],
        out_specs=(whole, whole),
        scratch_shapes=[
            pltpu.VMEM((CHUNKS, 8, 4, 6, 3, 2, ROWS, 128), bf16),
            pltpu.VMEM((4, 8, 2, 128), f32),
            pltpu.VMEM((3, 12, 12, 48, 128), bf16),
            pltpu.VMEM((3, 8, 8, 48, 128), f32),
            pltpu.VMEM((48, 8, 128), f32),
            pltpu.VMEM((4, 3, 48, 512), bf16),
            pltpu.VMEM((4, 144, 512), bf16),
            pltpu.VMEM((8, 3, 48, 512), bf16),
            pltpu.VMEM((2304, 48), f32),
            pltpu.VMEM((144, 144), f32),
            pltpu.VMEM((584, 48), f32),
            pltpu.VMEM((128, 8, 128), f32),
            pltpu.VMEM((128, 8, 128), f32),
            pltpu.VMEM((4, 48, 48), f32),
            pltpu.VMEM((4, 4, 48, 48), f32),
            dma((CHUNKS, 32)),
            dma((CHUNKS, 32)),
            dma((4,)),
            dma((4,)),
            dma((2, CHUNKS)),
            dma((2, CHUNKS)),
            dma((2,)),
            dma((2,)),
            dma((CHUNKS + 1,)),
            dma((128,)),
            dma((128,)),
            dma((4, 4)),
            dma((4, 4)),
            pltpu.SemaphoreType.REGULAR,
        ],
        compiler_params=pltpu.CompilerParams(
            collective_id=0, has_side_effects=True, vmem_limit_bytes=56 << 20
        ),
    )(modes, volume)


def solution(mesh):
    placed = (P("mode", None, "slab", None, None), P(None, ("mode", "slab"), None))
    return jax.shard_map(
        per_device,
        mesh=mesh,
        in_specs=placed,
        out_specs=(P(("mode", "slab"), None), P()),
        check_vma=False,
    )
```

```python
import functools
import math

import jax
import jax.numpy as jnp
from jax import lax
from jax.experimental import pallas as pl
from jax.experimental.pallas import tpu as pltpu
from jax.sharding import PartitionSpec as P

viscosity = 0.05
bf16 = jnp.bfloat16
f32 = jnp.float32
MESH = pl.DeviceIdType.MESH
NT = (((1,), (1,)), ((), ()))
GROUP = 24
CHUNKS = 4
ROWS = 8 // CHUNKS
AXES = ((3, 2), (0, 4), (1, 4), (2, 4))


def place():
    m = lax.axis_index("mode")
    s = lax.axis_index("slab")
    return s // 4, (m % 2) * 2 + (s % 4) // 2, m // 2, s % 2


def device(x, y, z, core):
    return (z * 2 + y // 2, x * 4 + (y % 2) * 2 + core)


def block_of(y, z, core):
    return 2 * (y * 4 + z + (y % 2) * (3 - 2 * z)) + core


def owner_of(q):
    step = q // 2
    y = step // 4
    along = step % 4
    return y, along + (y % 2) * (3 - 2 * along), q % 2


def lines_of(column, pair):
    return [(2 * column + plane, 2 * pair + row) for plane in range(2) for row in range(2)]


def slopes(b, column, pair, uc, vrecv, g, gw):
    for n, (plane, row) in enumerate(lines_of(column, pair)):
        weight = vrecv[pair, plane, n % 2, :].reshape(1, 128)
        lanes = slice(n * 128, n * 128 + 128)
        for a in range(3):

            def at(shift):
                dx, dy = (shift, 0) if b == 0 else (0, shift)
                return uc[a, plane + 2 + dx, row + 2 + dy].astype(f32)

            if b == 2:
                centre = at(0)
                m2, m1, p1, p2 = (pltpu.roll(centre, by, 1) for by in (2, 1, 127, 126))
            else:
                m2, m1, p1, p2 = at(-2), at(-1), at(1), at(2)
            rounded = (((m2 - p2) + 8.0 * (p1 - m1)) * (1.0 / 12.0)).astype(bf16)
            g[a, :, lanes] = rounded
            gw[a * 48 : a * 48 + 48, lanes] = (rounded.astype(f32) * weight).astype(bf16)


def products(modes_i, lines, uv, g):
    rows = []
    for i in modes_i:
        spread = [
            jnp.concatenate(
                [
                    jnp.broadcast_to(uv[a, plane, row, pl.ds(i, 1), :], (16, 128)).astype(bf16)
                    for plane, row in lines
                ],
                axis=1,
            )
            for a in range(3)
        ]
        for k in range(0, 48, 16):
            rows.append(
                spread[0] * g[0, k : k + 16, :]
                + spread[1] * g[1, k : k + 16, :]
                + spread[2] * g[2, k : k + 16, :]
            )
    return jnp.concatenate(rows, axis=0)


def advected(b, lines, uc):
    return jnp.concatenate([uc[b, plane + 2, row + 2] for plane, row in lines], axis=1)


def viscous(g, gw, diss):
    diss[...] += lax.dot_general(g[...].reshape(144, 512), gw[...], NT, preferred_element_type=f32)


def contract(b, column, pair, uc, uv, g, gw, conv, diss):
    lines = lines_of(column, pair)
    right = advected(b, lines, uc)
    for first in range(0, 48, GROUP):
        conv[first * 48 : (first + GROUP) * 48, :] += lax.dot_general(
            products(range(first, first + GROUP), lines, uv, g),
            right,
            NT,
            preferred_element_type=f32,
        )
    viscous(g, gw, diss)


def four_units(b, pair, uc, uv, vrecv, g, gw, conv, diss):
    slopes(b, 0, pair, uc, vrecv, g.at[0], gw.at[0])
    for n in range(4):
        if n < 3:
            slopes(b, n + 1, pair, uc, vrecv, g.at[n + 1], gw.at[n + 1])
        contract(b, n, pair, uc, uv, g.at[n], gw.at[n], conv, diss)


def main_kernel(
    scales, modes, volume, conv_out, diss_out,
    recv, vrecv, uc, uv, wide, g, gw, last_g, conv, diss, turned, pieces, rbuf, dsend, drecv,
    send_sem, recv_sem, vsend_sem, vrecv_sem, xsend_sem, xrecv_sem, ysend_sem, yrecv_sem, own_sem,
    psend_sem, precv_sem, dsend_sem, drecv_sem, ready_sem,
):
    x, y, z, core = place()
    m = lax.axis_index("mode")
    s = lax.axis_index("slab")
    t = s % 4
    q = block_of(y, z, core)
    number = m * 16 + s

    ys = [(y + dy) % 4 for dy in range(4)]
    zs = [(z + dz) % 4 for dz in range(4)]
    cores = [core, 1 - core]
    offsets = [(n * 11) % 32 for n in range(1, 32)]
    peers = []
    for off in offsets:
        py, pz, pc = ys[(off // 4) % 4], zs[off % 4], cores[off // 16]
        peers.append((8 * block_of(py, pz, pc), device(x, py, pz, pc)))

    def home(index):
        return (index,) + owner_of(4 * m + s // 4)

    def number_of(place_):
        ids = device(*place_)
        return ids[0] * 16 + ids[1]

    def source(part):
        return (q // 4, (q % 4) * 4 + part)

    neighbours = (
        (x > 0, (x - 1, y, z, core)),
        (x < 3, (x + 1, y, z, core)),
        (q > 0, (x,) + owner_of((q + 31) % 32)),
        (q < 31, (x,) + owner_of((q + 1) % 32)),
    )

    barrier = pltpu.get_barrier_semaphore()

    for _, other in peers:
        pl.semaphore_signal(barrier, inc=1, device_id=other, device_id_type=MESH)
    for step in range(1, 4):
        pl.semaphore_signal(
            barrier, inc=1, device_id=device((x + step) % 4, y, z, core), device_id_type=MESH
        )
    count = 34
    for index in range(4):
        target = home(index)
        other = number_of(target) != number

        @pl.when(other)
        def _():
            pl.semaphore_signal(barrier, inc=1, device_id=device(*target), device_id_type=MESH)

        origin = source(index)
        foreign = origin[0] * 16 + origin[1] != number

        @pl.when(foreign)
        def _():
            pl.semaphore_signal(barrier, inc=1, device_id=origin, device_id_type=MESH)

        count = count + other.astype(jnp.int32) + foreign.astype(jnp.int32)
    own_volume = number_of(home(x)) == number

    def volume_out(index):
        return pltpu.make_async_remote_copy(
            src_ref=volume.at[pl.ds(8 * index, 8)],
            dst_ref=vrecv.at[t],
            send_sem=vsend_sem.at[index],
            recv_sem=vrecv_sem.at[t],
            device_id=device(*home(index)),
            device_id_type=MESH,
        )

    def volume_own():
        return pltpu.make_async_copy(volume.at[pl.ds(8 * x, 8)], vrecv.at[t], own_sem.at[CHUNKS])

    def volume_in(part):
        return pltpu.make_async_remote_copy(
            src_ref=vrecv.at[part],
            dst_ref=vrecv.at[part],
            send_sem=vsend_sem.at[0],
            recv_sem=vrecv_sem.at[part],
            device_id=source(part),
            device_id_type=MESH,
        )

    def copy_out(chunk, first, other):
        rows = pl.multiple_of(first + ROWS * chunk, ROWS)
        return pltpu.make_async_remote_copy(
            src_ref=modes.at[:, :, :, pl.ds(rows, ROWS), :],
            dst_ref=recv.at[chunk, 4 * m + t],
            send_sem=send_sem.at[chunk],
            recv_sem=recv_sem.at[chunk],
            device_id=other,
            device_id_type=MESH,
        )

    def part_of(chunk):
        slots = recv.at[chunk, pl.ds(0, 31)]
        return pltpu.make_async_remote_copy(
            src_ref=slots,
            dst_ref=slots,
            send_sem=send_sem.at[chunk],
            recv_sem=recv_sem.at[chunk],
            device_id=peers[0][1],
            device_id_type=MESH,
        )

    def copy_own(chunk):
        first = pl.multiple_of(8 * q + ROWS * chunk, ROWS)
        return pltpu.make_async_copy(
            modes.at[:, :, :, pl.ds(first, ROWS), :], recv.at[chunk, 4 * m + t], own_sem.at[chunk]
        )

    @pl.when(own_volume)
    def _():
        volume_own().start()

    for chunk in range(CHUNKS):
        copy_own(chunk).start()

    edges = (uc.at[:, 0:2, 2:10], uc.at[:, 10:12, 2:10], uc.at[:, 2:10, 0:2], uc.at[:, 2:10, 10:12])
    for side in range(4):

        @pl.when(jnp.logical_not(neighbours[side][0]))
        def _():
            edges[side][...] = jnp.zeros(edges[side].shape, bf16)

    conv[...] = jnp.zeros_like(conv)
    diss[...] = jnp.zeros_like(diss)
    turned[576:, :] = jnp.zeros((8, 48), f32)
    pl.semaphore_wait(barrier, count)
    for step in range(1, 4):
        pl.semaphore_signal(
            ready_sem, inc=1, device_id=device((x + step) % 4, y, z, core), device_id_type=MESH
        )

    for index in range(4):
        other = number_of(home(index)) != number

        @pl.when(other)
        def _():
            volume_out(index).start()

    for chunk in range(CHUNKS):
        for first, other in peers:
            copy_out(chunk, first, other).start()

    for index in range(4):
        origin = source(index)
        foreign = origin[0] * 16 + origin[1] != number

        @pl.when(foreign)
        def _():
            volume_in(index).wait_recv()

    @pl.when(own_volume)
    def _():
        volume_own().wait()

    def x_copy(side, chunk):
        rows = pl.ds(2 + ROWS * chunk, ROWS)
        planes, there = ((2, 10), (8, 0))[side]
        return pltpu.make_async_remote_copy(
            src_ref=uc.at[:, planes : planes + 2, rows],
            dst_ref=uc.at[:, there : there + 2, rows],
            send_sem=xsend_sem.at[side, chunk],
            recv_sem=xrecv_sem.at[side, chunk],
            device_id=device(*neighbours[side][1]),
            device_id_type=MESH,
        )

    def x_arrival(side, chunk):
        rows = pl.ds(2 + ROWS * chunk, ROWS)
        there = (0, 10)[side]
        return pltpu.make_async_remote_copy(
            src_ref=uc.at[:, there : there + 2, rows],
            dst_ref=uc.at[:, there : there + 2, rows],
            send_sem=xsend_sem.at[1 - side, chunk],
            recv_sem=xrecv_sem.at[1 - side, chunk],
            device_id=device(*neighbours[side][1]),
            device_id_type=MESH,
        )

    def y_copy(side):
        rows, there = ((2, 10), (8, 0))[side]
        return pltpu.make_async_remote_copy(
            src_ref=uc.at[:, 2:10, rows : rows + 2],
            dst_ref=uc.at[:, 2:10, there : there + 2],
            send_sem=ysend_sem.at[side],
            recv_sem=yrecv_sem.at[side],
            device_id=device(*neighbours[2 + side][1]),
            device_id_type=MESH,
        )

    def y_arrival(side):
        there = (0, 10)[side]
        return pltpu.make_async_remote_copy(
            src_ref=uc.at[:, 2:10, there : there + 2],
            dst_ref=uc.at[:, 2:10, there : there + 2],
            send_sem=ysend_sem.at[1 - side],
            recv_sem=yrecv_sem.at[1 - side],
            device_id=device(*neighbours[2 + side][1]),
            device_id_type=MESH,
        )

    def arrive(chunk):
        part_of(chunk).wait_recv()
        copy_own(chunk).wait()

        def turn(n, _):
            a = n // 8
            plane = n % 8
            for six in range(8):
                wide[6 * six : 6 * six + 6, 0:ROWS, :] = recv[
                    chunk, 4 * six + plane // 2, :, a, plane % 2
                ].astype(f32)
            for row in range(ROWS):
                here = ROWS * chunk + row
                field = wide.reshape(384, 128)[pl.ds(row, 48, stride=8), :]
                uc[a, plane + 2, here + 2] = field.astype(bf16)
                weight = vrecv[here // 2, plane, pl.ds(here % 2, 1), :].reshape(1, 128)
                uv[a, plane, here] = field * weight
            return 0

        lax.fori_loop(0, 24, turn, 0)

        for side in range(2):

            @pl.when(neighbours[side][0])
            def _():
                x_copy(side, chunk).start()

        @pl.when(jnp.logical_and(chunk == 0, neighbours[2][0]))
        def _():
            y_copy(0).start()

        @pl.when(jnp.logical_and(chunk == CHUNKS - 1, neighbours[3][0]))
        def _():
            y_copy(1).start()

    def work(b, pair):
        four_units(b, pair, uc, uv, vrecv, g, gw, conv, diss)

    def advance(chunk, _):
        @pl.when(chunk < CHUNKS)
        def _():
            arrive(chunk)
            work(2, chunk)

        @pl.when(chunk >= 1)
        def _():
            for side in range(2):

                @pl.when(neighbours[side][0])
                def _():
                    x_arrival(side, chunk - 1).wait_recv()

            work(0, chunk - 1)

        @pl.when(chunk == 2)
        def _():
            work(1, 1)

        return 0

    lax.fori_loop(0, CHUNKS + 1, advance, 0)

    for side in range(2):

        @pl.when(neighbours[2 + side][0])
        def _():
            y_arrival(side).wait_recv()

    def last_slopes(part, _):
        pair = part + (part + 1) // 2
        for n in range(4):
            slot = last_g.at[4 * part + n]
            slopes(1, n, pair, uc, vrecv, slot, gw.at[n])
            viscous(slot, gw.at[n], diss)
        return 0

    lax.fori_loop(0, 3, last_slopes, 0)

    here = (x, y, z, core)

    def viscous_copy(phase, off, sign):
        axis, size = AXES[phase]
        there = list(here)
        there[axis] = (here[axis] + sign * off + size) % size
        slot = drecv.at[phase, here[axis] if sign > 0 else there[axis]]
        return pltpu.make_async_remote_copy(
            src_ref=dsend.at[phase] if sign > 0 else slot,
            dst_ref=slot,
            send_sem=dsend_sem.at[phase, off],
            recv_sem=drecv_sem.at[phase, off],
            device_id=device(*there),
            device_id_type=MESH,
        )

    def viscous_start(phase, total):
        dsend[phase] = total
        drecv[phase, here[AXES[phase][0]]] = total
        for off in range(1, AXES[phase][1]):
            viscous_copy(phase, off, 1).start()

    def viscous_end(phase):
        size = AXES[phase][1]
        for off in range(1, size):
            viscous_copy(phase, off, -1).wait_recv()
        total = drecv[phase, 0]
        for other in range(1, size):
            total = total + drecv[phase, other]
        return total

    viscous_start(0, diss[0:48, 0:48] + diss[48:96, 48:96] + diss[96:144, 96:144])
    pl.semaphore_wait(ready_sem, 3)

    me = number
    lane = lax.broadcasted_iota(jnp.int32, (8, 128), 1)
    line = lax.broadcasted_iota(jnp.int32, (8, 128), 0)

    def padded(first):
        return jnp.concatenate([turned[first : first + 8, :], jnp.zeros((8, 80), f32)], axis=1)

    def packed(first):
        tile = jnp.where(lane < 48, padded(first), pltpu.roll(padded(first + 8), 48, 1))
        for third in range(3):
            ends = pltpu.roll(padded(first + 16 - 2 * third), 96 - 16 * third, 1)
            tile = jnp.where((lane >= 96) & (lane < 112) & (line // 2 == third), ends, tile)
        return tile

    def piece_out(target, other):
        return pltpu.make_async_remote_copy(
            src_ref=pieces.at[target],
            dst_ref=rbuf.at[me],
            send_sem=psend_sem,
            recv_sem=precv_sem,
            device_id=other,
            device_id_type=MESH,
        )

    def all_pieces():
        return pltpu.make_async_remote_copy(
            src_ref=pieces.at[pl.ds(0, 127)],
            dst_ref=rbuf.at[pl.ds(0, 127)],
            send_sem=psend_sem,
            recv_sem=precv_sem,
            device_id=peers[0][1],
            device_id_type=MESH,
        )

    def triple_of(part, number_):
        return 4 * part + (part + number_) % 4

    def finish(number_, _):
        modes_i = [3 * triple_of(part, number_) + e for part in range(4) for e in range(3)]
        for n in range(12):
            lines = lines_of(n % 4, (0, 2, 3)[n // 4])
            sums = lax.dot_general(
                products(modes_i, lines, uv, last_g.at[n]),
                advected(1, lines, uc),
                NT,
                preferred_element_type=f32,
            )
            for part in range(4):
                first = pl.multiple_of(144 * triple_of(part, number_), 8)
                conv[pl.ds(first, 144), :] += sums[part * 144 : part * 144 + 144]
        for phase in range(4):

            @pl.when(number_ == phase)
            def _():
                total = viscous_end(phase)
                if phase < 3:
                    viscous_start(phase + 1, total)
                else:
                    diss_out[...] = total * scales[1]

        for part in range(4):
            for e in range(3):
                first = pl.multiple_of(144 * triple_of(part, number_) + 48 * e, 8)
                turned[part * 144 + e * 48 : part * 144 + e * 48 + 48, :] = jnp.transpose(
                    conv[pl.ds(first, 48), :]
                )
        for part in range(4):
            for r in range(8):
                pieces[8 * triple_of(part, number_) + r] = packed(part * 144 + 18 * r)

        for step in range(8):
            r = (s + step) % 8
            for part in range(4):
                triple = triple_of(zs[part], number_)
                target = 8 * triple + r

                @pl.when(target != me)
                def _():
                    piece_out(target, (triple // 2, 8 * (triple % 2) + r)).start()

                @pl.when(target == me)
                def _():
                    rbuf[me] = pieces[me]

        return 0

    lax.fori_loop(0, 4, finish, 0)

    all_pieces().wait_recv()

    def gather(n, running):
        return tuple(running[k] + rbuf[8 * n + k] for k in range(8))

    sums = lax.fori_loop(0, 16, gather, (jnp.zeros((8, 128), f32),) * 8)
    summed = sum(sums[1:], sums[0]) * scales[0]
    conv_out[0:8, :] = summed[:, :48]
    conv_out[8:16, :] = pltpu.roll(summed, 80, 1)[:, :48]
    ends = jnp.zeros((8, 128), f32)
    for third in range(3):
        piece = pltpu.roll(summed, 32 + 16 * third, 1)
        piece = pltpu.roll(piece, 8 - 2 * third, 0) if third else piece
        ends = jnp.where((lane >= 16 * third) & (lane < 16 * third + 16), piece, ends)
    conv_out[16:18, :] = ends[:2, :48]

    for chunk in range(CHUNKS):
        part_of(chunk).wait_send()
    for index in range(4):
        other = number_of(home(index)) != number

        @pl.when(other)
        def _():
            volume_out(index).wait_send()

    for side in range(2):

        @pl.when(neighbours[side][0])
        def _():
            for chunk in range(CHUNKS):
                x_copy(side, chunk).wait_send()

        @pl.when(neighbours[2 + side][0])
        def _():
            y_copy(side).wait_send()

    for phase in range(4):
        for off in range(1, AXES[phase][1]):
            viscous_copy(phase, off, 1).wait_send()

    all_pieces().wait_send()


def per_device(modes, volume):
    cell_total = 32 * 256 * 128
    scales = (1.0 / math.sqrt(cell_total), viscosity / cell_total)
    whole = pl.BlockSpec(memory_space=pltpu.VMEM)
    apart = pl.BlockSpec(memory_space=pl.ANY)
    dma = pltpu.SemaphoreType.DMA
    return pl.pallas_call(
        functools.partial(main_kernel, scales),
        out_shape=(
            jax.ShapeDtypeStruct((18, 48), f32),
            jax.ShapeDtypeStruct((48, 48), f32),
        ),
        in_specs=[apart, apart],
        out_specs=(whole, whole),
        scratch_shapes=[
            pltpu.VMEM((CHUNKS, 32, 6, 3, 2, ROWS, 128), bf16),
            pltpu.VMEM((4, 8, 2, 128), f32),
            pltpu.VMEM((3, 12, 12, 48, 128), bf16),
            pltpu.VMEM((3, 8, 8, 48, 128), f32),
            pltpu.VMEM((48, 8, 128), f32),
            pltpu.VMEM((4, 3, 48, 512), bf16),
            pltpu.VMEM((4, 144, 512), bf16),
            pltpu.VMEM((12, 3, 48, 512), bf16),
            pltpu.VMEM((2304, 48), f32),
            pltpu.VMEM((144, 144), f32),
            pltpu.VMEM((584, 48), f32),
            pltpu.VMEM((128, 8, 128), f32),
            pltpu.VMEM((128, 8, 128), f32),
            pltpu.VMEM((4, 48, 48), f32),
            pltpu.VMEM((4, 4, 48, 48), f32),
            dma((CHUNKS,)),
            dma((CHUNKS,)),
            dma((4,)),
            dma((4,)),
            dma((2, CHUNKS)),
            dma((2, CHUNKS)),
            dma((2,)),
            dma((2,)),
            dma((CHUNKS + 1,)),
            dma,
            dma,
            dma((4, 4)),
            dma((4, 4)),
            pltpu.SemaphoreType.REGULAR,
        ],
        compiler_params=pltpu.CompilerParams(
            collective_id=0, has_side_effects=True, vmem_limit_bytes=36 << 20
        ),
    )(modes, volume)


def solution(mesh):
    placed = (P("mode", None, "slab", None, None), P(None, ("mode", "slab"), None))
    return jax.shard_map(
        per_device,
        mesh=mesh,
        in_specs=placed,
        out_specs=(P(("mode", "slab"), None), P()),
        check_vma=False,
    )
```

```python
import functools
import math

import jax
import jax.numpy as jnp
from jax import lax
from jax.experimental import pallas as pl
from jax.experimental.pallas import tpu as pltpu
from jax.sharding import PartitionSpec as P

viscosity = 0.05
bf16 = jnp.bfloat16
f32 = jnp.float32
MESH = pl.DeviceIdType.MESH
NT = (((1,), (1,)), ((), ()))
GROUP = 24
CHUNKS = 4
ROWS = 8 // CHUNKS
AXES = ((3, 2), (0, 4), (1, 4), (2, 4))


def place():
    m = lax.axis_index("mode")
    s = lax.axis_index("slab")
    return s // 4, (m % 2) * 2 + (s % 4) // 2, m // 2, s % 2


def device(x, y, z, core):
    return (z * 2 + y // 2, x * 4 + (y % 2) * 2 + core)


def block_of(y, z, core):
    return 2 * (y * 4 + z + (y % 2) * (3 - 2 * z)) + core


def owner_of(q):
    step = q // 2
    y = step // 4
    along = step % 4
    return y, along + (y % 2) * (3 - 2 * along), q % 2


def lines_of(column, pair):
    return [(2 * column + plane, 2 * pair + row) for plane in range(2) for row in range(2)]


def slopes(b, column, pair, uc, vrecv, g, gw):
    for n, (plane, row) in enumerate(lines_of(column, pair)):
        weight = vrecv[pair, plane, n % 2, :].reshape(1, 128)
        lanes = slice(n * 128, n * 128 + 128)
        for a in range(3):

            def at(shift):
                dx, dy = (shift, 0) if b == 0 else (0, shift)
                return uc[a, plane + 2 + dx, row + 2 + dy].astype(f32)

            if b == 2:
                centre = at(0)
                m2, m1, p1, p2 = (pltpu.roll(centre, by, 1) for by in (2, 1, 127, 126))
            else:
                m2, m1, p1, p2 = at(-2), at(-1), at(1), at(2)
            rounded = (((m2 - p2) + 8.0 * (p1 - m1)) * (1.0 / 12.0)).astype(bf16)
            g[a, :, lanes] = rounded
            gw[a * 48 : a * 48 + 48, lanes] = (rounded.astype(f32) * weight).astype(bf16)


def products(modes_i, lines, uv, g):
    rows = []
    for i in modes_i:
        spread = [
            jnp.concatenate(
                [
                    jnp.broadcast_to(uv[a, plane, row, pl.ds(i, 1), :], (16, 128)).astype(bf16)
                    for plane, row in lines
                ],
                axis=1,
            )
            for a in range(3)
        ]
        for k in range(0, 48, 16):
            rows.append(
                spread[0] * g[0, k : k + 16, :]
                + spread[1] * g[1, k : k + 16, :]
                + spread[2] * g[2, k : k + 16, :]
            )
    return jnp.concatenate(rows, axis=0)


def advected(b, lines, uc):
    return jnp.concatenate([uc[b, plane + 2, row + 2] for plane, row in lines], axis=1)


def viscous(g, gw, diss):
    diss[...] += lax.dot_general(g[...].reshape(144, 512), gw[...], NT, preferred_element_type=f32)


def contract(b, column, pair, uc, uv, g, gw, conv, diss):
    lines = lines_of(column, pair)
    right = advected(b, lines, uc)
    for first in range(0, 48, GROUP):
        conv[first * 48 : (first + GROUP) * 48, :] += lax.dot_general(
            products(range(first, first + GROUP), lines, uv, g),
            right,
            NT,
            preferred_element_type=f32,
        )
    viscous(g, gw, diss)


def units(spots, uc, uv, vrecv, g, gw, conv, diss):
    slopes(*spots[0], uc, vrecv, g.at[0], gw.at[0])
    for n, spot in enumerate(spots):
        if n + 1 < len(spots):
            slopes(*spots[n + 1], uc, vrecv, g.at[n + 1], gw.at[n + 1])
        contract(*spot, uc, uv, g.at[n], gw.at[n], conv, diss)


def main_kernel(
    scales, modes, volume, conv_out, diss_out,
    recv, vrecv, uc, uv, wide, g, gw, last_g, conv, diss, turned, pieces, rbuf, dsend, drecv,
    send_sem, recv_sem, vsend_sem, vrecv_sem, xsend_sem, xrecv_sem, ysend_sem, yrecv_sem, own_sem,
    psend_sem, precv_sem, dsend_sem, drecv_sem, ready_sem,
):
    x, y, z, core = place()
    m = lax.axis_index("mode")
    s = lax.axis_index("slab")
    t = s % 4
    q = block_of(y, z, core)
    number = m * 16 + s

    ys = [(y + dy) % 4 for dy in range(4)]
    zs = [(z + dz) % 4 for dz in range(4)]
    cores = [core, 1 - core]
    offsets = [(n * 11) % 32 for n in range(1, 32)]
    peers = []
    for off in offsets:
        py, pz, pc = ys[(off // 4) % 4], zs[off % 4], cores[off // 16]
        peers.append((8 * block_of(py, pz, pc), device(x, py, pz, pc)))

    def home(index):
        return (index,) + owner_of(4 * m + s // 4)

    def number_of(place_):
        ids = device(*place_)
        return ids[0] * 16 + ids[1]

    def source(part):
        return (q // 4, (q % 4) * 4 + part)

    neighbours = (
        (x > 0, (x - 1, y, z, core)),
        (x < 3, (x + 1, y, z, core)),
        (q > 0, (x,) + owner_of((q + 31) % 32)),
        (q < 31, (x,) + owner_of((q + 1) % 32)),
    )

    barrier = pltpu.get_barrier_semaphore()

    for _, other in peers:
        pl.semaphore_signal(barrier, inc=1, device_id=other, device_id_type=MESH)
    for step in range(1, 4):
        pl.semaphore_signal(
            barrier, inc=1, device_id=device((x + step) % 4, y, z, core), device_id_type=MESH
        )
    count = 34
    for index in range(4):
        target = home(index)
        other = number_of(target) != number

        @pl.when(other)
        def _():
            pl.semaphore_signal(barrier, inc=1, device_id=device(*target), device_id_type=MESH)

        origin = source(index)
        foreign = origin[0] * 16 + origin[1] != number

        @pl.when(foreign)
        def _():
            pl.semaphore_signal(barrier, inc=1, device_id=origin, device_id_type=MESH)

        count = count + other.astype(jnp.int32) + foreign.astype(jnp.int32)
    own_volume = number_of(home(x)) == number

    def volume_out(index):
        return pltpu.make_async_remote_copy(
            src_ref=volume.at[pl.ds(8 * index, 8)],
            dst_ref=vrecv.at[t],
            send_sem=vsend_sem.at[index],
            recv_sem=vrecv_sem.at[t],
            device_id=device(*home(index)),
            device_id_type=MESH,
        )

    def volume_own():
        return pltpu.make_async_copy(volume.at[pl.ds(8 * x, 8)], vrecv.at[t], own_sem.at[CHUNKS])

    def volume_in(part):
        return pltpu.make_async_remote_copy(
            src_ref=vrecv.at[part],
            dst_ref=vrecv.at[part],
            send_sem=vsend_sem.at[0],
            recv_sem=vrecv_sem.at[part],
            device_id=source(part),
            device_id_type=MESH,
        )

    def copy_out(chunk, first, other):
        rows = pl.multiple_of(first + ROWS * chunk, ROWS)
        return pltpu.make_async_remote_copy(
            src_ref=modes.at[:, :, :, pl.ds(rows, ROWS), :],
            dst_ref=recv.at[chunk, 4 * m + t],
            send_sem=send_sem.at[chunk],
            recv_sem=recv_sem.at[chunk],
            device_id=other,
            device_id_type=MESH,
        )

    def part_of(chunk):
        slots = recv.at[chunk, pl.ds(0, 31)]
        return pltpu.make_async_remote_copy(
            src_ref=slots,
            dst_ref=slots,
            send_sem=send_sem.at[chunk],
            recv_sem=recv_sem.at[chunk],
            device_id=peers[0][1],
            device_id_type=MESH,
        )

    def copy_own(chunk):
        first = pl.multiple_of(8 * q + ROWS * chunk, ROWS)
        return pltpu.make_async_copy(
            modes.at[:, :, :, pl.ds(first, ROWS), :], recv.at[chunk, 4 * m + t], own_sem.at[chunk]
        )

    @pl.when(own_volume)
    def _():
        volume_own().start()

    for chunk in range(CHUNKS):
        copy_own(chunk).start()

    edges = (uc.at[:, 0:2, 2:10], uc.at[:, 10:12, 2:10], uc.at[:, 2:10, 0:2], uc.at[:, 2:10, 10:12])
    for side in range(4):

        @pl.when(jnp.logical_not(neighbours[side][0]))
        def _():
            edges[side][...] = jnp.zeros(edges[side].shape, bf16)

    conv[...] = jnp.zeros_like(conv)
    diss[...] = jnp.zeros_like(diss)
    turned[576:, :] = jnp.zeros((8, 48), f32)
    pl.semaphore_wait(barrier, count)
    for step in range(1, 4):
        pl.semaphore_signal(
            ready_sem, inc=1, device_id=device((x + step) % 4, y, z, core), device_id_type=MESH
        )

    for index in range(4):
        other = number_of(home(index)) != number

        @pl.when(other)
        def _():
            volume_out(index).start()

    for chunk in range(CHUNKS):
        for first, other in peers:
            copy_out(chunk, first, other).start()

    for index in range(4):
        origin = source(index)
        foreign = origin[0] * 16 + origin[1] != number

        @pl.when(foreign)
        def _():
            volume_in(index).wait_recv()

    @pl.when(own_volume)
    def _():
        volume_own().wait()

    def x_copy(side, chunk):
        rows = pl.ds(2 + ROWS * chunk, ROWS)
        planes, there = ((2, 10), (8, 0))[side]
        return pltpu.make_async_remote_copy(
            src_ref=uc.at[:, planes : planes + 2, rows],
            dst_ref=uc.at[:, there : there + 2, rows],
            send_sem=xsend_sem.at[side, chunk],
            recv_sem=xrecv_sem.at[side, chunk],
            device_id=device(*neighbours[side][1]),
            device_id_type=MESH,
        )

    def x_arrival(side, chunk):
        rows = pl.ds(2 + ROWS * chunk, ROWS)
        there = (0, 10)[side]
        return pltpu.make_async_remote_copy(
            src_ref=uc.at[:, there : there + 2, rows],
            dst_ref=uc.at[:, there : there + 2, rows],
            send_sem=xsend_sem.at[1 - side, chunk],
            recv_sem=xrecv_sem.at[1 - side, chunk],
            device_id=device(*neighbours[side][1]),
            device_id_type=MESH,
        )

    def y_copy(side):
        rows, there = ((2, 10), (8, 0))[side]
        return pltpu.make_async_remote_copy(
            src_ref=uc.at[:, 2:10, rows : rows + 2],
            dst_ref=uc.at[:, 2:10, there : there + 2],
            send_sem=ysend_sem.at[side],
            recv_sem=yrecv_sem.at[side],
            device_id=device(*neighbours[2 + side][1]),
            device_id_type=MESH,
        )

    def y_arrival(side):
        there = (0, 10)[side]
        return pltpu.make_async_remote_copy(
            src_ref=uc.at[:, 2:10, there : there + 2],
            dst_ref=uc.at[:, 2:10, there : there + 2],
            send_sem=ysend_sem.at[1 - side],
            recv_sem=yrecv_sem.at[1 - side],
            device_id=device(*neighbours[2 + side][1]),
            device_id_type=MESH,
        )

    def arrive(chunk):
        part_of(chunk).wait_recv()
        copy_own(chunk).wait()

        def turn(plane, _):
            for a in range(3):
                for six in range(8):
                    wide[a, 6 * six : 6 * six + 6, 0:ROWS, :] = recv[
                        chunk, 4 * six + plane // 2, :, a, plane % 2
                    ].astype(f32)
            for a in range(3):
                for row in range(ROWS):
                    here = ROWS * chunk + row
                    field = wide.at[a].reshape(384, 128)[pl.ds(row, 48, stride=8), :]
                    uc[a, plane + 2, here + 2] = field.astype(bf16)
                    weight = vrecv[here // 2, plane, pl.ds(here % 2, 1), :].reshape(1, 128)
                    uv[a, plane, here] = field * weight
            return 0

        lax.fori_loop(0, 8, turn, 0)

        for side in range(2):

            @pl.when(neighbours[side][0])
            def _():
                x_copy(side, chunk).start()

        @pl.when(jnp.logical_and(chunk == 0, neighbours[2][0]))
        def _():
            y_copy(0).start()

        @pl.when(jnp.logical_and(chunk == CHUNKS - 1, neighbours[3][0]))
        def _():
            y_copy(1).start()

    def work(*spots):
        units(spots, uc, uv, vrecv, g, gw, conv, diss)

    def advance(chunk, _):
        @pl.when(chunk < CHUNKS)
        def _():
            arrive(chunk)
            work(*[(2, column, chunk) for column in range(4)], (0, 1, chunk), (0, 2, chunk))

        @pl.when(chunk >= 1)
        def _():
            for side in range(2):

                @pl.when(neighbours[side][0])
                def _():
                    x_arrival(side, chunk - 1).wait_recv()

            work((0, 0, chunk - 1), (0, 3, chunk - 1))

        @pl.when(chunk == 2)
        def _():
            work(*[(1, column, 1) for column in range(4)])

        return 0

    lax.fori_loop(0, CHUNKS + 1, advance, 0)

    for side in range(2):

        @pl.when(neighbours[2 + side][0])
        def _():
            y_arrival(side).wait_recv()

    def last_slopes(part, _):
        pair = part + (part + 1) // 2
        for n in range(4):
            slot = last_g.at[4 * part + n]
            slopes(1, n, pair, uc, vrecv, slot, gw.at[n])
            viscous(slot, gw.at[n], diss)
        return 0

    lax.fori_loop(0, 3, last_slopes, 0)

    here = (x, y, z, core)

    def viscous_copy(phase, off, sign):
        axis, size = AXES[phase]
        there = list(here)
        there[axis] = (here[axis] + sign * off + size) % size
        slot = drecv.at[phase, here[axis] if sign > 0 else there[axis]]
        return pltpu.make_async_remote_copy(
            src_ref=dsend.at[phase] if sign > 0 else slot,
            dst_ref=slot,
            send_sem=dsend_sem.at[phase, off],
            recv_sem=drecv_sem.at[phase, off],
            device_id=device(*there),
            device_id_type=MESH,
        )

    def viscous_start(phase, total):
        dsend[phase] = total
        drecv[phase, here[AXES[phase][0]]] = total
        for off in range(1, AXES[phase][1]):
            viscous_copy(phase, off, 1).start()

    def viscous_end(phase):
        size = AXES[phase][1]
        for off in range(1, size):
            viscous_copy(phase, off, -1).wait_recv()
        total = drecv[phase, 0]
        for other in range(1, size):
            total = total + drecv[phase, other]
        return total

    viscous_start(0, diss[0:48, 0:48] + diss[48:96, 48:96] + diss[96:144, 96:144])
    pl.semaphore_wait(ready_sem, 3)

    me = number
    lane = lax.broadcasted_iota(jnp.int32, (8, 128), 1)
    line = lax.broadcasted_iota(jnp.int32, (8, 128), 0)

    def padded(first):
        return jnp.concatenate([turned[first : first + 8, :], jnp.zeros((8, 80), f32)], axis=1)

    def packed(first):
        tile = jnp.where(lane < 48, padded(first), pltpu.roll(padded(first + 8), 48, 1))
        for third in range(3):
            ends = pltpu.roll(padded(first + 16 - 2 * third), 96 - 16 * third, 1)
            tile = jnp.where((lane >= 96) & (lane < 112) & (line // 2 == third), ends, tile)
        return tile

    def piece_out(target, other):
        return pltpu.make_async_remote_copy(
            src_ref=pieces.at[target],
            dst_ref=rbuf.at[me],
            send_sem=psend_sem,
            recv_sem=precv_sem,
            device_id=other,
            device_id_type=MESH,
        )

    def all_pieces():
        return pltpu.make_async_remote_copy(
            src_ref=pieces.at[pl.ds(0, 127)],
            dst_ref=rbuf.at[pl.ds(0, 127)],
            send_sem=psend_sem,
            recv_sem=precv_sem,
            device_id=peers[0][1],
            device_id_type=MESH,
        )

    def triple_of(part, number_):
        return 4 * part + (part + number_) % 4

    def finish(number_, _):
        modes_i = [3 * triple_of(part, number_) + e for part in range(4) for e in range(3)]
        for n in range(12):
            lines = lines_of(n % 4, (0, 2, 3)[n // 4])
            sums = lax.dot_general(
                products(modes_i, lines, uv, last_g.at[n]),
                advected(1, lines, uc),
                NT,
                preferred_element_type=f32,
            )
            for part in range(4):
                first = pl.multiple_of(144 * triple_of(part, number_), 8)
                conv[pl.ds(first, 144), :] += sums[part * 144 : part * 144 + 144]
        for phase in range(4):

            @pl.when(number_ == phase)
            def _():
                total = viscous_end(phase)
                if phase < 3:
                    viscous_start(phase + 1, total)
                else:
                    diss_out[...] = total * scales[1]

        for part in range(4):
            for e in range(3):
                first = pl.multiple_of(144 * triple_of(part, number_) + 48 * e, 8)
                turned[part * 144 + e * 48 : part * 144 + e * 48 + 48, :] = jnp.transpose(
                    conv[pl.ds(first, 48), :]
                )
        for part in range(4):
            for r in range(8):
                pieces[8 * triple_of(part, number_) + r] = packed(part * 144 + 18 * r)

        for step in range(8):
            r = (s + step) % 8
            for part in range(4):
                triple = triple_of(zs[part], number_)
                target = 8 * triple + r

                @pl.when(target != me)
                def _():
                    piece_out(target, (triple // 2, 8 * (triple % 2) + r)).start()

                @pl.when(target == me)
                def _():
                    rbuf[me] = pieces[me]

        return 0

    lax.fori_loop(0, 4, finish, 0)

    all_pieces().wait_recv()

    def gather(n, running):
        return tuple(running[k] + rbuf[8 * n + k] for k in range(8))

    sums = lax.fori_loop(0, 16, gather, (jnp.zeros((8, 128), f32),) * 8)
    summed = sum(sums[1:], sums[0]) * scales[0]
    conv_out[0:8, :] = summed[:, :48]
    conv_out[8:16, :] = pltpu.roll(summed, 80, 1)[:, :48]
    ends = jnp.zeros((8, 128), f32)
    for third in range(3):
        piece = pltpu.roll(summed, 32 + 16 * third, 1)
        piece = pltpu.roll(piece, 8 - 2 * third, 0) if third else piece
        ends = jnp.where((lane >= 16 * third) & (lane < 16 * third + 16), piece, ends)
    conv_out[16:18, :] = ends[:2, :48]

    for chunk in range(CHUNKS):
        part_of(chunk).wait_send()
    for index in range(4):
        other = number_of(home(index)) != number

        @pl.when(other)
        def _():
            volume_out(index).wait_send()

    for side in range(2):

        @pl.when(neighbours[side][0])
        def _():
            for chunk in range(CHUNKS):
                x_copy(side, chunk).wait_send()

        @pl.when(neighbours[2 + side][0])
        def _():
            y_copy(side).wait_send()

    for phase in range(4):
        for off in range(1, AXES[phase][1]):
            viscous_copy(phase, off, 1).wait_send()

    all_pieces().wait_send()


def per_device(modes, volume):
    cell_total = 32 * 256 * 128
    scales = (1.0 / math.sqrt(cell_total), viscosity / cell_total)
    whole = pl.BlockSpec(memory_space=pltpu.VMEM)
    apart = pl.BlockSpec(memory_space=pl.ANY)
    dma = pltpu.SemaphoreType.DMA
    return pl.pallas_call(
        functools.partial(main_kernel, scales),
        out_shape=(
            jax.ShapeDtypeStruct((18, 48), f32),
            jax.ShapeDtypeStruct((48, 48), f32),
        ),
        in_specs=[apart, apart],
        out_specs=(whole, whole),
        scratch_shapes=[
            pltpu.VMEM((CHUNKS, 32, 6, 3, 2, ROWS, 128), bf16),
            pltpu.VMEM((4, 8, 2, 128), f32),
            pltpu.VMEM((3, 12, 12, 48, 128), bf16),
            pltpu.VMEM((3, 8, 8, 48, 128), f32),
            pltpu.VMEM((3, 48, 8, 128), f32),
            pltpu.VMEM((6, 3, 48, 512), bf16),
            pltpu.VMEM((6, 144, 512), bf16),
            pltpu.VMEM((12, 3, 48, 512), bf16),
            pltpu.VMEM((2304, 48), f32),
            pltpu.VMEM((144, 144), f32),
            pltpu.VMEM((584, 48), f32),
            pltpu.VMEM((128, 8, 128), f32),
            pltpu.VMEM((128, 8, 128), f32),
            pltpu.VMEM((4, 48, 48), f32),
            pltpu.VMEM((4, 4, 48, 48), f32),
            dma((CHUNKS,)),
            dma((CHUNKS,)),
            dma((4,)),
            dma((4,)),
            dma((2, CHUNKS)),
            dma((2, CHUNKS)),
            dma((2,)),
            dma((2,)),
            dma((CHUNKS + 1,)),
            dma,
            dma,
            dma((4, 4)),
            dma((4, 4)),
            pltpu.SemaphoreType.REGULAR,
        ],
        compiler_params=pltpu.CompilerParams(
            collective_id=0, has_side_effects=True, vmem_limit_bytes=53 << 20
        ),
    )(modes, volume)


def solution(mesh):
    placed = (P("mode", None, "slab", None, None), P(None, ("mode", "slab"), None))
    return jax.shard_map(
        per_device,
        mesh=mesh,
        in_specs=placed,
        out_specs=(P(("mode", "slab"), None), P()),
        check_vma=False,
    )
```

```python
import functools
import math

import jax
import jax.numpy as jnp
from jax import lax
from jax.experimental import pallas as pl
from jax.experimental.pallas import tpu as pltpu
from jax.sharding import PartitionSpec as P

viscosity = 0.05
bf16 = jnp.bfloat16
f32 = jnp.float32
MESH = pl.DeviceIdType.MESH
NT = (((1,), (1,)), ((), ()))
GROUP = 24
CHUNKS = 4
ROWS = 8 // CHUNKS
AXES = ((3, 2), (0, 4), (1, 4), (2, 4))


def place():
    m = lax.axis_index("mode")
    s = lax.axis_index("slab")
    return s // 4, (m % 2) * 2 + (s % 4) // 2, m // 2, s % 2


def device(x, y, z, core):
    return (z * 2 + y // 2, x * 4 + (y % 2) * 2 + core)


def block_of(y, z, core):
    return 2 * (y * 4 + z + (y % 2) * (3 - 2 * z)) + core


def owner_of(q):
    step = q // 2
    y = step // 4
    along = step % 4
    return y, along + (y % 2) * (3 - 2 * along), q % 2


def lines_of(column, pair):
    return [(2 * column + plane, 2 * pair + row) for plane in range(2) for row in range(2)]


def slopes(b, column, pair, uc, vrecv, g, gw):
    for n, (plane, row) in enumerate(lines_of(column, pair)):
        weight = vrecv[pair, plane, n % 2, :].reshape(1, 128)
        lanes = slice(n * 128, n * 128 + 128)
        for a in range(3):

            def at(shift):
                dx, dy = (shift, 0) if b == 0 else (0, shift)
                return uc[a, plane + 2 + dx, row + 2 + dy].astype(f32)

            if b == 2:
                centre = at(0)
                m2, m1, p1, p2 = (pltpu.roll(centre, by, 1) for by in (2, 1, 127, 126))
            else:
                m2, m1, p1, p2 = at(-2), at(-1), at(1), at(2)
            rounded = (((m2 - p2) + 8.0 * (p1 - m1)) * (1.0 / 12.0)).astype(bf16)
            g[a, :, lanes] = rounded
            gw[a * 48 : a * 48 + 48, lanes] = (rounded.astype(f32) * weight).astype(bf16)


def products(modes_i, lines, uv, g):
    rows = []
    for i in modes_i:
        spread = [
            jnp.concatenate(
                [
                    jnp.broadcast_to(uv[a, plane, row, pl.ds(i, 1), :], (16, 128)).astype(bf16)
                    for plane, row in lines
                ],
                axis=1,
            )
            for a in range(3)
        ]
        for k in range(0, 48, 16):
            rows.append(
                spread[0] * g[0, k : k + 16, :]
                + spread[1] * g[1, k : k + 16, :]
                + spread[2] * g[2, k : k + 16, :]
            )
    return jnp.concatenate(rows, axis=0)


def advected(b, lines, uc):
    return jnp.concatenate([uc[b, plane + 2, row + 2] for plane, row in lines], axis=1)


def viscous(g, gw, diss):
    diss[...] += lax.dot_general(g[...].reshape(144, 512), gw[...], NT, preferred_element_type=f32)


def contract(b, column, pair, uc, uv, g, gw, conv, diss):
    lines = lines_of(column, pair)
    right = advected(b, lines, uc)
    for first in range(0, 48, GROUP):
        conv[first * 48 : (first + GROUP) * 48, :] += lax.dot_general(
            products(range(first, first + GROUP), lines, uv, g),
            right,
            NT,
            preferred_element_type=f32,
        )
    viscous(g, gw, diss)


def units(spots, uc, uv, vrecv, g, gw, conv, diss):
    slopes(*spots[0], uc, vrecv, g.at[0], gw.at[0])
    for n, spot in enumerate(spots):
        if n + 1 < len(spots):
            slopes(*spots[n + 1], uc, vrecv, g.at[n + 1], gw.at[n + 1])
        contract(*spot, uc, uv, g.at[n], gw.at[n], conv, diss)


def main_kernel(
    scales, modes, volume, conv_out, diss_out,
    recv, vrecv, uc, uv, wide, g, gw, last_g, conv, diss, turned, pieces, rbuf, dsend, drecv,
    send_sem, recv_sem, vsend_sem, vrecv_sem, xsend_sem, xrecv_sem, ysend_sem, yrecv_sem, own_sem,
    psend_sem, precv_sem, dsend_sem, drecv_sem, ready_sem,
):
    x, y, z, core = place()
    m = lax.axis_index("mode")
    s = lax.axis_index("slab")
    t = s % 4
    q = block_of(y, z, core)
    number = m * 16 + s

    ys = [(y + dy) % 4 for dy in range(4)]
    zs = [(z + dz) % 4 for dz in range(4)]
    cores = [core, 1 - core]
    offsets = [(n * 11) % 32 for n in range(1, 32)]
    peers = []
    for off in offsets:
        py, pz, pc = ys[(off // 4) % 4], zs[off % 4], cores[off // 16]
        peers.append((8 * block_of(py, pz, pc), device(x, py, pz, pc)))

    def home(index):
        return (index,) + owner_of(4 * m + s // 4)

    def number_of(place_):
        ids = device(*place_)
        return ids[0] * 16 + ids[1]

    def source(part):
        return (q // 4, (q % 4) * 4 + part)

    neighbours = (
        (x > 0, (x - 1, y, z, core)),
        (x < 3, (x + 1, y, z, core)),
        (q > 0, (x,) + owner_of((q + 31) % 32)),
        (q < 31, (x,) + owner_of((q + 1) % 32)),
    )

    barrier = pltpu.get_barrier_semaphore()

    for _, other in peers:
        pl.semaphore_signal(barrier, inc=1, device_id=other, device_id_type=MESH)
    for step in range(1, 4):
        pl.semaphore_signal(
            barrier, inc=1, device_id=device((x + step) % 4, y, z, core), device_id_type=MESH
        )
    count = 34
    for index in range(4):
        target = home(index)
        other = number_of(target) != number

        @pl.when(other)
        def _():
            pl.semaphore_signal(barrier, inc=1, device_id=device(*target), device_id_type=MESH)

        origin = source(index)
        foreign = origin[0] * 16 + origin[1] != number

        @pl.when(foreign)
        def _():
            pl.semaphore_signal(barrier, inc=1, device_id=origin, device_id_type=MESH)

        count = count + other.astype(jnp.int32) + foreign.astype(jnp.int32)
    own_volume = number_of(home(x)) == number

    def volume_out(index):
        return pltpu.make_async_remote_copy(
            src_ref=volume.at[pl.ds(8 * index, 8)],
            dst_ref=vrecv.at[t],
            send_sem=vsend_sem.at[index],
            recv_sem=vrecv_sem.at[t],
            device_id=device(*home(index)),
            device_id_type=MESH,
        )

    def volume_own():
        return pltpu.make_async_copy(volume.at[pl.ds(8 * x, 8)], vrecv.at[t], own_sem.at[CHUNKS])

    def volume_in(part):
        return pltpu.make_async_remote_copy(
            src_ref=vrecv.at[part],
            dst_ref=vrecv.at[part],
            send_sem=vsend_sem.at[0],
            recv_sem=vrecv_sem.at[part],
            device_id=source(part),
            device_id_type=MESH,
        )

    def copy_out(chunk, first, other):
        rows = pl.multiple_of(first + ROWS * chunk, ROWS)
        return pltpu.make_async_remote_copy(
            src_ref=modes.at[:, :, :, pl.ds(rows, ROWS), :],
            dst_ref=recv.at[chunk, 4 * m + t],
            send_sem=send_sem.at[chunk],
            recv_sem=recv_sem.at[chunk],
            device_id=other,
            device_id_type=MESH,
        )

    def part_of(chunk):
        slots = recv.at[chunk, pl.ds(0, 31)]
        return pltpu.make_async_remote_copy(
            src_ref=slots,
            dst_ref=slots,
            send_sem=send_sem.at[chunk],
            recv_sem=recv_sem.at[chunk],
            device_id=peers[0][1],
            device_id_type=MESH,
        )

    def copy_own(chunk):
        first = pl.multiple_of(8 * q + ROWS * chunk, ROWS)
        return pltpu.make_async_copy(
            modes.at[:, :, :, pl.ds(first, ROWS), :], recv.at[chunk, 4 * m + t], own_sem.at[chunk]
        )

    @pl.when(own_volume)
    def _():
        volume_own().start()

    for chunk in range(CHUNKS):
        copy_own(chunk).start()

    edges = (uc.at[:, 0:2, 2:10], uc.at[:, 10:12, 2:10], uc.at[:, 2:10, 0:2], uc.at[:, 2:10, 10:12])
    for side in range(4):

        @pl.when(jnp.logical_not(neighbours[side][0]))
        def _():
            edges[side][...] = jnp.zeros(edges[side].shape, bf16)

    conv[...] = jnp.zeros_like(conv)
    diss[...] = jnp.zeros_like(diss)
    turned[576:, :] = jnp.zeros((8, 48), f32)
    pl.semaphore_wait(barrier, count)
    for step in range(1, 4):
        pl.semaphore_signal(
            ready_sem, inc=1, device_id=device((x + step) % 4, y, z, core), device_id_type=MESH
        )

    for first, other in peers:
        copy_out(0, first, other).start()

    for index in range(4):
        other = number_of(home(index)) != number

        @pl.when(other)
        def _():
            volume_out(index).start()

    for chunk in range(1, CHUNKS):
        for first, other in peers:
            copy_out(chunk, first, other).start()

    for index in range(4):
        origin = source(index)
        foreign = origin[0] * 16 + origin[1] != number

        @pl.when(foreign)
        def _():
            volume_in(index).wait_recv()

    @pl.when(own_volume)
    def _():
        volume_own().wait()

    def x_copy(side, chunk):
        rows = pl.ds(2 + ROWS * chunk, ROWS)
        planes, there = ((2, 10), (8, 0))[side]
        return pltpu.make_async_remote_copy(
            src_ref=uc.at[:, planes : planes + 2, rows],
            dst_ref=uc.at[:, there : there + 2, rows],
            send_sem=xsend_sem.at[side, chunk],
            recv_sem=xrecv_sem.at[side, chunk],
            device_id=device(*neighbours[side][1]),
            device_id_type=MESH,
        )

    def x_arrival(side, chunk):
        rows = pl.ds(2 + ROWS * chunk, ROWS)
        there = (0, 10)[side]
        return pltpu.make_async_remote_copy(
            src_ref=uc.at[:, there : there + 2, rows],
            dst_ref=uc.at[:, there : there + 2, rows],
            send_sem=xsend_sem.at[1 - side, chunk],
            recv_sem=xrecv_sem.at[1 - side, chunk],
            device_id=device(*neighbours[side][1]),
            device_id_type=MESH,
        )

    def y_copy(side):
        rows, there = ((2, 10), (8, 0))[side]
        return pltpu.make_async_remote_copy(
            src_ref=uc.at[:, 2:10, rows : rows + 2],
            dst_ref=uc.at[:, 2:10, there : there + 2],
            send_sem=ysend_sem.at[side],
            recv_sem=yrecv_sem.at[side],
            device_id=device(*neighbours[2 + side][1]),
            device_id_type=MESH,
        )

    def y_arrival(side):
        there = (0, 10)[side]
        return pltpu.make_async_remote_copy(
            src_ref=uc.at[:, 2:10, there : there + 2],
            dst_ref=uc.at[:, 2:10, there : there + 2],
            send_sem=ysend_sem.at[1 - side],
            recv_sem=yrecv_sem.at[1 - side],
            device_id=device(*neighbours[2 + side][1]),
            device_id_type=MESH,
        )

    def arrive(chunk):
        part_of(chunk).wait_recv()
        copy_own(chunk).wait()

        def turn(plane, _):
            for a in range(3):
                for six in range(8):
                    wide[a, 6 * six : 6 * six + 6, 0:ROWS, :] = recv[
                        chunk, 4 * six + plane // 2, :, a, plane % 2
                    ].astype(f32)
            for a in range(3):
                for row in range(ROWS):
                    here = ROWS * chunk + row
                    field = wide.at[a].reshape(384, 128)[pl.ds(row, 48, stride=8), :]
                    uc[a, plane + 2, here + 2] = field.astype(bf16)
                    weight = vrecv[here // 2, plane, pl.ds(here % 2, 1), :].reshape(1, 128)
                    uv[a, plane, here] = field * weight
            return 0

        lax.fori_loop(0, 8, turn, 0)

        for side in range(2):

            @pl.when(neighbours[side][0])
            def _():
                x_copy(side, chunk).start()

        @pl.when(jnp.logical_and(chunk == 0, neighbours[2][0]))
        def _():
            y_copy(0).start()

        @pl.when(jnp.logical_and(chunk == CHUNKS - 1, neighbours[3][0]))
        def _():
            y_copy(1).start()

    def work(*spots):
        units(spots, uc, uv, vrecv, g, gw, conv, diss)

    def advance(chunk, _):
        @pl.when(chunk < CHUNKS)
        def _():
            arrive(chunk)
            work(*[(2, column, chunk) for column in range(4)], (0, 1, chunk), (0, 2, chunk))

        @pl.when(chunk >= 1)
        def _():
            for side in range(2):

                @pl.when(neighbours[side][0])
                def _():
                    x_arrival(side, chunk - 1).wait_recv()

            work((0, 0, chunk - 1), (0, 3, chunk - 1))

        @pl.when(chunk == 2)
        def _():
            work(*[(1, column, 1) for column in range(4)])

        return 0

    lax.fori_loop(0, CHUNKS + 1, advance, 0)

    def last_slopes(*parts):
        for n in range(4 * len(parts)):
            part = parts[n // 4]
            slot = last_g.at[4 * part + n % 4]
            slopes(1, n % 4, (0, 2, 3)[part], uc, vrecv, slot, gw.at[n % 6])
            viscous(slot, gw.at[n % 6], diss)

    last_slopes(1)
    for side in range(2):

        @pl.when(neighbours[2 + side][0])
        def _():
            y_arrival(side).wait_recv()

    last_slopes(0, 2)

    here = (x, y, z, core)

    def viscous_copy(phase, off, sign):
        axis, size = AXES[phase]
        there = list(here)
        there[axis] = (here[axis] + sign * off + size) % size
        slot = drecv.at[phase, here[axis] if sign > 0 else there[axis]]
        return pltpu.make_async_remote_copy(
            src_ref=dsend.at[phase] if sign > 0 else slot,
            dst_ref=slot,
            send_sem=dsend_sem.at[phase, off],
            recv_sem=drecv_sem.at[phase, off],
            device_id=device(*there),
            device_id_type=MESH,
        )

    def viscous_start(phase, total):
        dsend[phase] = total
        drecv[phase, here[AXES[phase][0]]] = total
        for off in range(1, AXES[phase][1]):
            viscous_copy(phase, off, 1).start()

    def viscous_end(phase):
        size = AXES[phase][1]
        for off in range(1, size):
            viscous_copy(phase, off, -1).wait_recv()
        total = drecv[phase, 0]
        for other in range(1, size):
            total = total + drecv[phase, other]
        return total

    viscous_start(0, diss[0:48, 0:48] + diss[48:96, 48:96] + diss[96:144, 96:144])
    pl.semaphore_wait(ready_sem, 3)

    me = number
    lane = lax.broadcasted_iota(jnp.int32, (8, 128), 1)
    line = lax.broadcasted_iota(jnp.int32, (8, 128), 0)

    def padded(first):
        return jnp.concatenate([turned[first : first + 8, :], jnp.zeros((8, 80), f32)], axis=1)

    def packed(first):
        tile = jnp.where(lane < 48, padded(first), pltpu.roll(padded(first + 8), 48, 1))
        for third in range(3):
            ends = pltpu.roll(padded(first + 16 - 2 * third), 96 - 16 * third, 1)
            tile = jnp.where((lane >= 96) & (lane < 112) & (line // 2 == third), ends, tile)
        return tile

    def piece_out(target, other):
        return pltpu.make_async_remote_copy(
            src_ref=pieces.at[target],
            dst_ref=rbuf.at[me],
            send_sem=psend_sem,
            recv_sem=precv_sem,
            device_id=other,
            device_id_type=MESH,
        )

    def all_pieces():
        return pltpu.make_async_remote_copy(
            src_ref=pieces.at[pl.ds(0, 127)],
            dst_ref=rbuf.at[pl.ds(0, 127)],
            send_sem=psend_sem,
            recv_sem=precv_sem,
            device_id=peers[0][1],
            device_id_type=MESH,
        )

    def triple_of(part, number_):
        return 4 * part + (part + number_) % 4

    def finish(number_, _):
        modes_i = [3 * triple_of(part, number_) + e for part in range(4) for e in range(3)]
        for n in range(12):
            lines = lines_of(n % 4, (0, 2, 3)[n // 4])
            sums = lax.dot_general(
                products(modes_i, lines, uv, last_g.at[n]),
                advected(1, lines, uc),
                NT,
                preferred_element_type=f32,
            )
            for part in range(4):
                first = pl.multiple_of(144 * triple_of(part, number_), 8)
                conv[pl.ds(first, 144), :] += sums[part * 144 : part * 144 + 144]
        for phase in range(4):

            @pl.when(number_ == phase)
            def _():
                total = viscous_end(phase)
                if phase < 3:
                    viscous_start(phase + 1, total)
                else:
                    diss_out[...] = total * scales[1]

        for part in range(4):
            for e in range(3):
                first = pl.multiple_of(144 * triple_of(part, number_) + 48 * e, 8)
                turned[part * 144 + e * 48 : part * 144 + e * 48 + 48, :] = jnp.transpose(
                    conv[pl.ds(first, 48), :]
                )
        for part in range(4):
            for r in range(8):
                pieces[8 * triple_of(part, number_) + r] = packed(part * 144 + 18 * r)

        for step in range(8):
            r = (s + step) % 8
            for part in range(4):
                triple = triple_of(zs[part], number_)
                target = 8 * triple + r

                @pl.when(target != me)
                def _():
                    piece_out(target, (triple // 2, 8 * (triple % 2) + r)).start()

                @pl.when(target == me)
                def _():
                    rbuf[me] = pieces[me]

        return 0

    lax.fori_loop(0, 4, finish, 0)

    all_pieces().wait_recv()

    def gather(n, running):
        return tuple(running[k] + rbuf[8 * n + k] for k in range(8))

    sums = lax.fori_loop(0, 16, gather, (jnp.zeros((8, 128), f32),) * 8)
    summed = sum(sums[1:], sums[0]) * scales[0]
    conv_out[0:8, :] = summed[:, :48]
    conv_out[8:16, :] = pltpu.roll(summed, 80, 1)[:, :48]
    ends = jnp.zeros((8, 128), f32)
    for third in range(3):
        piece = pltpu.roll(summed, 32 + 16 * third, 1)
        piece = pltpu.roll(piece, 8 - 2 * third, 0) if third else piece
        ends = jnp.where((lane >= 16 * third) & (lane < 16 * third + 16), piece, ends)
    conv_out[16:18, :] = ends[:2, :48]

    for chunk in range(CHUNKS):
        part_of(chunk).wait_send()
    for index in range(4):
        other = number_of(home(index)) != number

        @pl.when(other)
        def _():
            volume_out(index).wait_send()

    for side in range(2):

        @pl.when(neighbours[side][0])
        def _():
            for chunk in range(CHUNKS):
                x_copy(side, chunk).wait_send()

        @pl.when(neighbours[2 + side][0])
        def _():
            y_copy(side).wait_send()

    for phase in range(4):
        for off in range(1, AXES[phase][1]):
            viscous_copy(phase, off, 1).wait_send()

    all_pieces().wait_send()


def per_device(modes, volume):
    cell_total = 32 * 256 * 128
    scales = (1.0 / math.sqrt(cell_total), viscosity / cell_total)
    whole = pl.BlockSpec(memory_space=pltpu.VMEM)
    apart = pl.BlockSpec(memory_space=pl.ANY)
    dma = pltpu.SemaphoreType.DMA
    return pl.pallas_call(
        functools.partial(main_kernel, scales),
        out_shape=(
            jax.ShapeDtypeStruct((18, 48), f32),
            jax.ShapeDtypeStruct((48, 48), f32),
        ),
        in_specs=[apart, apart],
        out_specs=(whole, whole),
        scratch_shapes=[
            pltpu.VMEM((CHUNKS, 32, 6, 3, 2, ROWS, 128), bf16),
            pltpu.VMEM((4, 8, 2, 128), f32),
            pltpu.VMEM((3, 12, 12, 48, 128), bf16),
            pltpu.VMEM((3, 8, 8, 48, 128), f32),
            pltpu.VMEM((3, 48, 8, 128), f32),
            pltpu.VMEM((6, 3, 48, 512), bf16),
            pltpu.VMEM((6, 144, 512), bf16),
            pltpu.VMEM((12, 3, 48, 512), bf16),
            pltpu.VMEM((2304, 48), f32),
            pltpu.VMEM((144, 144), f32),
            pltpu.VMEM((584, 48), f32),
            pltpu.VMEM((128, 8, 128), f32),
            pltpu.VMEM((128, 8, 128), f32),
            pltpu.VMEM((4, 48, 48), f32),
            pltpu.VMEM((4, 4, 48, 48), f32),
            dma((CHUNKS,)),
            dma((CHUNKS,)),
            dma((4,)),
            dma((4,)),
            dma((2, CHUNKS)),
            dma((2, CHUNKS)),
            dma((2,)),
            dma((2,)),
            dma((CHUNKS + 1,)),
            dma,
            dma,
            dma((4, 4)),
            dma((4, 4)),
            pltpu.SemaphoreType.REGULAR,
        ],
        compiler_params=pltpu.CompilerParams(
            collective_id=0, has_side_effects=True, vmem_limit_bytes=53 << 20
        ),
    )(modes, volume)


def solution(mesh):
    placed = (P("mode", None, "slab", None, None), P(None, ("mode", "slab"), None))
    return jax.shard_map(
        per_device,
        mesh=mesh,
        in_specs=placed,
        out_specs=(P(("mode", "slab"), None), P()),
        check_vma=False,
    )
```
